32 devices in a mesh: ens: 2 (over x), lat: 16 (over z, y, core).
Axes of the slice: x: 2, y: 2, z: 4, core: 2. Of those that a mesh axis runs over, the one named last changes fastest.
Arguments:
- atmos: bfloat16 [11520, 1024], P(('ens', 'lat')), parts along dimension 0, may hold values from -6 to 6
- ocean_state: bfloat16 [76, 128, 1440], P(None, ('ens', 'lat')), parts along dimension 1, may hold values from -6 to 6
- land_mask: int32 [64, 1440], P('lat'), may hold values 0 or 1
- w_qkv: bfloat16 [1024, 3072], replicated, may hold values from -0.1875 to 0.1875
- w_out: bfloat16 [1024, 1024], replicated, may hold values from -0.1875 to 0.1875
- head_scale: float32 [16], replicated, may hold values from 0.5 to 80
- gain_attn: float32 [1024], replicated, may hold values from 0.5 to 1.5
- gain_flux: float32 [1024], replicated, may hold values from 0.1 to 1.9
- w_flux: bfloat16 [1024, 16], replicated, may hold values from -0.1875 to 0.1875
- surf_embed: float32 [4, 1024], replicated, may hold values from -3 to 3
- flux_start: int32 [64], P('lat'), may hold values from 0 to 14, as said below
- flux_weight: float32 [64, 2], P('lat'), may hold values from 0.25 to 1
- surf_start: int32 [16], P('lat'), may hold values from -2 to 59, as said below
- surf_weight: float32 [16, 7], P('lat'), may hold values from 0.1 to 0.5
- conv_first: bfloat16 [9, 128, 92], replicated, may hold values from -0.21875 to 0.21875
- conv_second: bfloat16 [9, 76, 128], replicated, may hold values from -0.1875 to 0.1875
Outputs:
- atmos_next: bfloat16 [11520, 1024], P(('ens', 'lat')), parts along dimension 0
- ocean_next: bfloat16 [76, 128, 1440], P(None, ('ens', 'lat')), parts along dimension 1
The draws below stay inside these ranges and needn't reach their ends.
There are 2 independent parts, one for each index of `ens`. The reference program is written for one: setup_inputs(seed, part) draws one part's arguments, and reference() takes and returns one part's arrays. A program takes and returns all parts, laid end to end along the dimension named above; an argument that names none is the same for every part. Nothing has to cross between parts.
Inputs may be any that keep to these rules, and one draw needn't show every extreme that they name: flux_start[i] is i // 4 - 1 or i // 4, kept within 0 to 14. surf_start[r] is 4 r - 2 or 4 r - 1.
All inputs are finite; a program needn't handle non-finite values. No bound on the sum of `land_mask` on one device may be relied on, other than what follows from the above.
Results may differ from the reference program's by a relative error of at most 0.0065.
The reference program's roundings to bfloat16 on the way count: a program that leaves them out, or rounds other values in their place, can miss the bound.
Values may be sent and summed in bfloat16 or wider, within the bound.
A program may use at most 128 MiB of HBM per device.

```python
import jax
import jax.numpy as jnp
from jax import lax

D = 1024
HEADS = 16
NFLUX = 16
LEVELS = 19
VARS = 4
OCH = 76
HID = 128
ALON = 360
SPAN = 4
OLON = 1440
RATIO = 4
AROWS = 16
OROWS = 64
TOKENS = 5760
FBAND = 2
OBAND = 7
OSTEPS = 2


def draw_head_scale(key, part):
    lowest = jnp.log(jnp.float32(0.5))
    highest = jnp.log(jnp.float32(2.5))
    moderate = jnp.exp(jax.random.uniform(key, (HEADS,), jnp.float32, lowest, highest))
    return moderate


def draw_flux_start(key, part):
    ocean_rows = jnp.arange(OROWS, dtype=jnp.int32)
    jitter = jax.random.randint(key, (OROWS,), 0, 2, dtype=jnp.int32)
    return jnp.clip(ocean_rows // RATIO - 1 + jitter, 0, AROWS - FBAND).astype(jnp.int32)


def draw_surf_start(key, part):
    centres = jnp.arange(AROWS, dtype=jnp.int32) * RATIO
    jitter = jax.random.randint(key, (AROWS,), 0, 2, dtype=jnp.int32)
    return (centres - 2 + jitter).astype(jnp.int32)


def touch_ends(entries, rng, least, top_value):
    place = [jax.random.randint(jax.random.fold_in(rng, axis), (), 0, length) for axis, length in enumerate(entries.shape)]
    widest = entries.shape.index(max(entries.shape))
    beside = place[:widest] + [(place[widest] + 1) % entries.shape[widest]] + place[widest + 1:]
    return entries.at[tuple(place)].set(least).at[tuple(beside)].set(top_value)


def block_scale(rng, shape, cuts, smallest, top_value):
    loudness = 1.0
    for axis_at, shards_of in cuts:
        draws = jax.random.uniform(jax.random.fold_in(jax.random.fold_in(rng, 6), axis_at), (shards_of,), jnp.float32, smallest / len(cuts), top_value / len(cuts))
        loudness = loudness * jnp.repeat(jnp.exp(draws), shape[axis_at] // shards_of).reshape((-1,) + (1,) * (len(shape) - 1 - axis_at))
    return loudness


def bell_draw(stream_key, dims, scale, most, shards=(), held_as=jnp.bfloat16):
    loudness = block_scale(stream_key, dims, shards, -0.22, 0.18) if shards else 1.0
    entries = jax.random.normal(stream_key, dims, jnp.float32) * scale * loudness
    return jnp.minimum(jnp.maximum(entries, -most), most).astype(held_as)


def setup_inputs(seed: int = 0, part: int = 0) -> dict:
    seeds = jax.random.split(jax.random.key(seed), 17)
    part_splits = jax.random.split(jax.random.fold_in(seeds[16], part), 17)
    return {
        "atmos": bell_draw(part_splits[0], (TOKENS, D), 1.0, 6.0, ((0, 16),)),
        "ocean_state": bell_draw(part_splits[1], (OCH, OROWS, OLON), 1.0, 6.0, ((1, 16),)),
        "land_mask": touch_ends((jax.random.randint(seeds[2], (OROWS, OLON), 0, 10) < 7).astype(jnp.int32), jax.random.fold_in(seeds[2], 1), 0, 1),
        "w_qkv": bell_draw(seeds[3], (D, 3 * D), D ** -0.5, 0.1875),
        "w_out": bell_draw(seeds[4], (D, D), D ** -0.5, 0.1875),
        "head_scale": draw_head_scale(jax.random.fold_in(seeds[16], 71), part),
        "gain_attn": jnp.clip(1.0 + 0.1 * jax.random.normal(seeds[6], (D,), jnp.float32), 0.5, 1.5),
        "gain_flux": jnp.clip(1.0 + 0.18 * jax.random.normal(seeds[7], (D,), jnp.float32), 0.1, 1.9),
        "w_flux": bell_draw(seeds[8], (D, NFLUX), D ** -0.5, 0.1875),
        "surf_embed": bell_draw(seeds[9], (VARS, D), VARS ** -0.5, 3.0, (), jnp.float32),
        "flux_start": draw_flux_start(jax.random.fold_in(seeds[16], 71), part),
        "flux_weight": jnp.clip(0.25 + 0.75 * jax.random.uniform(seeds[11], (OROWS, FBAND), jnp.float32) ** block_scale(seeds[11], (OROWS, FBAND), ((0, 16),), -0.2, 0.2), 0.25, 1.0),
        "surf_start": draw_surf_start(jax.random.fold_in(seeds[16], 71), part),
        "surf_weight": jnp.clip(0.1 + 0.4 * jax.random.uniform(seeds[13], (AROWS, OBAND), jnp.float32) ** block_scale(seeds[13], (AROWS, OBAND), ((0, 16),), -0.2, 0.2), 0.1, 0.5),
        "conv_first": bell_draw(seeds[14], (9, HID, OCH + NFLUX), (9 * (OCH + NFLUX)) ** -0.5, 0.21875),
        "conv_second": bell_draw(seeds[15], (9, OCH, HID), (9 * HID) ** -0.5, 0.1875),
    }


def rms_norm(values, scaling):
    return values * lax.rsqrt(lax.optimization_barrier(jnp.mean(values * values, axis=-1, keepdims=True)) + 1e-06) * scaling

def band_matrix(starts, weight, first_col, col_count):
    columns = first_col + jnp.arange(col_count, dtype=jnp.int32)
    summed = jnp.zeros((starts.shape[0], col_count), jnp.float32)
    for offset in range(weight.shape[1]):
        matches = (columns[None, :] == starts[:, None] + offset).astype(jnp.float32)
        summed = summed + weight[:, offset:offset + 1] * matches
    return summed

def surface_rows(ocean_now):
    fields = ocean_now[0::LEVELS]
    averaged = lax.optimization_barrier(jnp.mean(fields.reshape(fields.shape[0], fields.shape[1], fields.shape[2] // SPAN, SPAN), axis=3))
    return averaged.transpose(1, 0, 2).reshape(fields.shape[1], -1)

def head_parts(qkv, head_scale):
    token_count = qkv.shape[0]
    width = qkv.shape[1] // 3
    head_count = head_scale.shape[0]
    depth = width // head_count
    query_raw = qkv[:, :width].reshape(token_count, head_count, depth)
    key_raw = qkv[:, width:2 * width].reshape(token_count, head_count, depth)
    query_part = query_raw * lax.rsqrt(lax.optimization_barrier(jnp.mean(query_raw * query_raw, axis=-1, keepdims=True)) + 1e-06)
    query_part = query_part * (head_scale[None, :, None] / jnp.sqrt(jnp.float32(depth)))
    key_part = key_raw * lax.rsqrt(lax.optimization_barrier(jnp.mean(key_raw * key_raw, axis=-1, keepdims=True)) + 1e-06)
    value_part = qkv[:, 2 * width:]
    return (query_part.astype(jnp.bfloat16), key_part.astype(jnp.bfloat16), value_part.astype(jnp.bfloat16))

def attend(query_rows, key_rows, value_rows, valid):
    key_count = key_rows.shape[0]
    scores = jnp.einsum('qhd,khd->hqk', query_rows.astype(jnp.float32), key_rows.astype(jnp.float32))
    scores = jnp.where(valid[None, None, :], scores, -1e+30)
    largest = lax.optimization_barrier(jnp.max(scores, axis=2, keepdims=True))
    raised = jnp.exp(scores - largest)
    probs = (raised / lax.optimization_barrier(jnp.sum(raised, axis=2, keepdims=True))).astype(jnp.bfloat16)
    value_heads = value_rows.reshape(key_count, key_rows.shape[1], key_rows.shape[2])
    mixed = jnp.einsum('hqk,khd->qhd', probs.astype(jnp.float32), value_heads.astype(jnp.float32))
    return mixed.astype(jnp.bfloat16).reshape(query_rows.shape[0], -1)

def spread_flux(regridded, flux_count):
    row_count = regridded.shape[0]
    shaped = regridded.reshape(row_count, -1, flux_count).transpose(2, 0, 1)
    return jnp.repeat(shaped, SPAN, axis=2).astype(jnp.bfloat16)

def convolve(padded, weight, row_count):
    channels = padded.shape[0]
    lon_count = padded.shape[2]
    summed = jnp.zeros((weight.shape[1], row_count * lon_count), jnp.float32)
    for tap_index in range(9):
        row_step = tap_index // 3 - 1
        lon_step = tap_index % 3 - 1
        shifted = jnp.roll(padded[:, 1 + row_step:1 + row_step + row_count, :], -lon_step, axis=2)
        summed = summed + jnp.dot(weight[tap_index], shifted.reshape(channels, -1), preferred_element_type=jnp.float32)
    return summed.reshape(weight.shape[1], row_count, lon_count)

def pad_rows(fields):
    return jnp.pad(fields, ((0, 0), (1, 1), (0, 0)))

def reference(atmos, ocean_state, land_mask, w_qkv, w_out, head_scale, gain_attn, gain_flux, w_flux, surf_embed, flux_start, flux_weight, surf_start, surf_weight, conv_first, conv_second):
    ocean_now = ocean_state.astype(jnp.float32)
    surface = surface_rows(ocean_now).astype(jnp.bfloat16)
    surf_matrix = band_matrix(surf_start, surf_weight, 0, OROWS)
    surf_atm = jnp.dot(surf_matrix, surface.astype(jnp.float32), precision=lax.Precision.HIGHEST)
    surf_tokens = surf_atm.reshape(AROWS, VARS, ALON).transpose(0, 2, 1).reshape(AROWS * ALON, VARS)
    start = atmos.astype(jnp.float32) + jnp.dot(surf_tokens, surf_embed, precision=lax.Precision.HIGHEST)
    normed = rms_norm(start, gain_attn).astype(jnp.bfloat16)
    qkv = jnp.dot(normed, w_qkv, preferred_element_type=jnp.float32)
    query_part, key_part, value_part = head_parts(qkv, head_scale)
    head_count = query_part.shape[1]
    depth = query_part.shape[2]
    query_grid = query_part.reshape(AROWS, ALON, head_count, depth)
    key_grid = jnp.pad(key_part.reshape(AROWS, ALON, head_count, depth), ((1, 1), (0, 0), (0, 0), (0, 0)))
    value_grid = jnp.pad(value_part.reshape(AROWS, ALON, D), ((1, 1), (0, 0), (0, 0)))

    def one_row(row_id):
        query_rows = lax.dynamic_slice_in_dim(query_grid, row_id, 1, 0)[0]
        key_rows = lax.dynamic_slice_in_dim(key_grid, row_id, 3, 0).reshape(3 * ALON, head_count, depth)
        value_rows = lax.dynamic_slice_in_dim(value_grid, row_id, 3, 0).reshape(3 * ALON, D)
        global_rows = row_id - 1 + jnp.arange(3 * ALON, dtype=jnp.int32) // ALON
        valid = (global_rows >= 0) & (global_rows < AROWS)
        return attend(query_rows, key_rows, value_rows, valid)
    mixed = lax.map(one_row, jnp.arange(AROWS, dtype=jnp.int32)).reshape(AROWS * ALON, D)
    after = start + jnp.dot(mixed, w_out, preferred_element_type=jnp.float32)
    atmos_next = after.astype(jnp.bfloat16)
    flux_in = rms_norm(after, gain_flux).astype(jnp.bfloat16)
    fluxes = jnp.dot(flux_in, w_flux, preferred_element_type=jnp.float32).astype(jnp.bfloat16).reshape(AROWS, ALON * NFLUX)
    flux_matrix = band_matrix(flux_start, flux_weight, 0, AROWS)
    regridded = jnp.dot(flux_matrix, fluxes.astype(jnp.float32), precision=lax.Precision.HIGHEST)
    ocean_flux = spread_flux(regridded, NFLUX)
    sea_cells = land_mask.astype(jnp.float32)
    for step_index in range(OSTEPS):
        inputs = jnp.concatenate([ocean_now.astype(jnp.bfloat16), ocean_flux], axis=0)
        hidden = jax.nn.gelu(convolve(pad_rows(inputs), conv_first, OROWS), approximate=True).astype(jnp.bfloat16)
        ocean_now = ocean_now + sea_cells[None] * convolve(pad_rows(hidden), conv_second, OROWS)
    return (atmos_next, ocean_now.astype(jnp.bfloat16))
```

```python
import jax
import jax.numpy as jnp
from jax import lax
from jax.experimental import pallas as pl
from jax.experimental.pallas import tpu as pltpu
from jax.sharding import PartitionSpec as P

LEVELS = 19
VARS = 4
SPAN = 4
OSTEPS = 2


def padded_2(block, sides, width):
    for axis, dim in sides:
        count = lax.axis_size(axis)
        forward = [(i, i + 1) for i in range(count - 1)]
        backward = [(target, source) for source, target in forward]
        low = lax.ppermute(
            lax.slice_in_dim(block, block.shape[dim] - width, None, axis=dim), axis, forward
        )
        high = lax.ppermute(lax.slice_in_dim(block, 0, width, axis=dim), axis, backward)
        block = jnp.concatenate([low, block, high], axis=dim)
    return block


def rms_norm(values, scaling):
    return values * lax.rsqrt(jnp.mean(values * values, axis=-1, keepdims=True) + 1e-06) * scaling


def band_matrix(starts, weight, first_col, col_count):
    columns = first_col + jnp.arange(col_count, dtype=jnp.int32)
    summed = jnp.zeros((starts.shape[0], col_count), jnp.float32)
    for offset in range(weight.shape[1]):
        matches = (columns[None, :] == starts[:, None] + offset).astype(jnp.float32)
        summed = summed + weight[:, offset : offset + 1] * matches
    return summed


def surface_rows(ocean_now):
    fields = ocean_now[0::LEVELS]
    averaged = jnp.mean(
        fields.reshape(fields.shape[0], fields.shape[1], fields.shape[2] // SPAN, SPAN), axis=3
    )
    return averaged.transpose(1, 0, 2).reshape(fields.shape[1], -1)


def norm_keys(key_raw, head_count):
    token_count = key_raw.shape[0]
    shaped = key_raw.reshape(token_count, head_count, -1)
    normed = shaped * lax.rsqrt(jnp.mean(shaped * shaped, axis=-1, keepdims=True) + 1e-06)
    return normed.astype(jnp.bfloat16).reshape(token_count, -1)


def attend(query_rows, key_rows, value_rows, valid):
    key_count = key_rows.shape[0]
    scores = jnp.einsum("qhd,khd->hqk", query_rows, key_rows, preferred_element_type=jnp.float32)
    scores = jnp.where(valid[None, None, :], scores, -1e30)
    largest = jnp.max(scores, axis=2, keepdims=True)
    raised = jnp.exp(scores - largest)
    probs = (raised / jnp.sum(raised, axis=2, keepdims=True)).astype(jnp.bfloat16)
    value_heads = value_rows.reshape(key_count, key_rows.shape[1], key_rows.shape[2])
    mixed = jnp.einsum("hqk,khd->qhd", probs, value_heads, preferred_element_type=jnp.float32)
    return mixed.astype(jnp.bfloat16).reshape(query_rows.shape[0], -1)


def ocean_kernel(pos_ref, mat_ref, low_ref, mid_ref, high_ref, mask_ref, flux_ref, spread_ref,
                 first_ref, second_ref, out_ref, xs, hs, st):
    och = mid_ref.shape[1]
    olon = mid_ref.shape[2]
    orows = mid_ref.shape[0]
    wide = xs.shape[1]
    nflux = flux_ref.shape[1]
    spread_rows = flux_ref.shape[0]
    hid = first_ref.shape[0] // 3
    opad = second_ref.shape[0] // 3
    stride = opad + nflux
    first_row = pos_ref[0]
    total = pos_ref[1]
    tail = wide - 128
    first_pad = olon - tail

    def wrap(head, last):
        lane = lax.broadcasted_iota(jnp.int32, last.shape, 1)
        end = pltpu.roll(last, 128 - first_pad, 1)
        begin = pltpu.roll(head, first_pad, 1)
        return jnp.where(lane == first_pad, begin, jnp.where(lane == 127, end, last))

    def combine(full, size):
        left = pltpu.roll(full[0:size], 1, 1)
        right = pltpu.roll(full[2 * size : 3 * size], wide - 1, 1)
        return left + full[size : 2 * size] + right

    for part, ref in enumerate((low_ref, mid_ref, high_ref)):
        def fill(i, carry, ref=ref, part=part):
            row = part * orows + i
            state = ref[i].astype(jnp.float32)
            state = jnp.concatenate([state, jnp.zeros((opad - och, olon), jnp.float32)], axis=0)
            last = jnp.concatenate(
                [state[:, tail:], jnp.zeros((opad, wide - olon), jnp.float32)], axis=1
            )
            st[row, :, 0:tail] = state[:, 0:tail]
            st[row, :, tail:] = wrap(state[:, 0:128], last)
            base = pl.multiple_of(row * stride, 16)
            xs[pl.ds(base, opad), :] = st[row].astype(jnp.bfloat16)
            return carry
        lax.fori_loop(0, orows, fill, 0)

    def regrid(row, carry):
        total_flux = mat_ref[row, 0] * flux_ref[0].astype(jnp.float32)
        for r in range(1, spread_rows):
            total_flux = total_flux + mat_ref[row, r] * flux_ref[r].astype(jnp.float32)
        rows = jnp.dot(total_flux.astype(jnp.bfloat16), spread_ref[...],
                       preferred_element_type=jnp.float32)
        base = pl.multiple_of(row * stride + opad, 16)
        xs[pl.ds(base, nflux), :] = rows.astype(jnp.bfloat16)
        return carry
    lax.fori_loop(0, 3 * orows, regrid, 0)

    for step in range(OSTEPS):
        edge = 1 + 2 * step

        def first(row, carry):
            block = xs[pl.ds(pl.multiple_of((row - 1) * stride, 16), 3 * stride), :]
            full = jnp.dot(first_ref[...], block, preferred_element_type=jnp.float32)
            hidden = jax.nn.gelu(combine(full, hid), approximate=True)
            place = first_row + row - orows
            inside = jnp.where((place >= 0) & (place < total), 1.0, 0.0).astype(jnp.float32)
            hidden = hidden * inside
            base = pl.multiple_of(row * hid, 16)
            hs[pl.ds(base, hid), 0:tail] = hidden[:, 0:tail].astype(jnp.bfloat16)
            hs[pl.ds(base, hid), tail:] = wrap(hidden[:, 0:128], hidden[:, tail:]).astype(jnp.bfloat16)
            return carry
        lax.fori_loop(edge, 3 * orows - edge, first, 0)

        def second(row, carry):
            block = hs[pl.ds(pl.multiple_of((row - 1) * hid, 16), 3 * hid), :]
            full = jnp.dot(second_ref[...], block, preferred_element_type=jnp.float32)
            state = st[row] + mask_ref[row] * combine(full, opad)
            if step == OSTEPS - 1:
                out_ref[row - orows] = state[0:och, 0:olon].astype(jnp.bfloat16)
            else:
                st[row, :, 0:tail] = state[:, 0:tail]
                st[row, :, tail:] = wrap(state[:, 0:128], state[:, tail:])
                base = pl.multiple_of(row * stride, 16)
                xs[pl.ds(base, opad), :] = st[row].astype(jnp.bfloat16)
            return carry
        lax.fori_loop(edge + 1, 3 * orows - edge - 1, second, 0)


def round_up(value, unit):
    return (value + unit - 1) // unit * unit


def ocean_steps(state_parts, mask, fluxes, matrix, conv_first, conv_second, position, band_count):
    orows, och, olon = state_parts[1].shape
    nflux = fluxes.shape[1]
    hid = conv_first.shape[1]
    opad = round_up(och, 16)
    wide = round_up(olon + 2, 128)
    alon = fluxes.shape[2]
    first = conv_first.reshape(3, 3, hid, och + nflux)
    first = jnp.concatenate(
        [first[..., :och], jnp.zeros((3, 3, hid, opad - och), first.dtype), first[..., och:]], axis=3
    )
    first = first.transpose(1, 2, 0, 3).reshape(3 * hid, 3 * (opad + nflux))
    second = jnp.pad(conv_second.reshape(3, 3, och, hid), ((0, 0), (0, 0), (0, opad - och), (0, 0)))
    second = second.transpose(1, 2, 0, 3).reshape(3 * opad, 3 * hid)
    column = jnp.arange(wide, dtype=jnp.int32)
    longitude = jnp.where(column < olon, column, jnp.where(column == olon, 0, olon - 1))
    spread = (longitude[None, :] // SPAN == jnp.arange(alon, dtype=jnp.int32)[:, None]).astype(jnp.bfloat16)
    scalars = jnp.stack([position * orows, band_count * orows]).astype(jnp.int32)
    mask = jnp.pad(mask.astype(jnp.float32), ((0, 0), (0, wide - olon)))[:, None, :]
    vmem = pl.BlockSpec(memory_space=pltpu.VMEM)
    smem = pl.BlockSpec(memory_space=pltpu.SMEM)
    return pl.pallas_call(
        ocean_kernel,
        out_shape=jax.ShapeDtypeStruct((orows, och, olon), jnp.bfloat16),
        in_specs=[smem, smem] + [vmem] * 8,
        out_specs=vmem,
        scratch_shapes=[
            pltpu.VMEM((3 * orows * (opad + nflux), wide), jnp.bfloat16),
            pltpu.VMEM((3 * orows * hid, wide), jnp.bfloat16),
            pltpu.VMEM((3 * orows, opad, wide), jnp.float32),
        ],
        compiler_params=pltpu.CompilerParams(vmem_limit_bytes=60 * 1024 * 1024),
        name="ocean_steps",
    )(scalars, matrix, *state_parts, mask, fluxes, spread, first, second)


def shifted(block, offset):
    count = lax.axis_size("lat")
    pairs = [(i, i + offset) for i in range(count) if 0 <= i + offset < count]
    return lax.ppermute(block, "lat", pairs)


def local(
    atmos,
    ocean_state,
    land_mask,
    w_qkv,
    w_out,
    head_scale,
    gain_attn,
    gain_flux,
    w_flux,
    surf_embed,
    flux_start,
    flux_weight,
    surf_start,
    surf_weight,
    conv_first,
    conv_second,
):
    position = lax.axis_index("lat")
    band_count = lax.axis_size("lat")
    ocean_now = ocean_state.astype(jnp.float32)
    orows = ocean_now.shape[1]
    olon = ocean_now.shape[2]
    alon = olon // SPAN
    arows = atmos.shape[0] // alon
    width = atmos.shape[1]
    head_count = head_scale.shape[0]
    depth = width // head_count
    flux_count = w_flux.shape[1]
    surface = surface_rows(ocean_now).astype(jnp.bfloat16)
    surf_near = padded_2(surface, (("lat", 0),), 2)
    surf_matrix = band_matrix(surf_start, surf_weight, position * orows - 2, orows + 4)
    surf_atm = jnp.dot(surf_matrix, surf_near.astype(jnp.float32), precision=lax.Precision.HIGHEST)
    surf_tokens = surf_atm.reshape(arows, VARS, alon).transpose(0, 2, 1).reshape(arows * alon, VARS)
    start = atmos.astype(jnp.float32) + jnp.dot(
        surf_tokens, surf_embed, precision=lax.Precision.HIGHEST
    )
    normed = rms_norm(start, gain_attn).astype(jnp.bfloat16)
    qkv = jnp.dot(normed, w_qkv, preferred_element_type=jnp.float32)
    token_count = qkv.shape[0]
    query_raw = qkv[:, :width].reshape(token_count, head_count, depth)
    query_part = query_raw * lax.rsqrt(
        jnp.mean(query_raw * query_raw, axis=-1, keepdims=True) + 1e-06
    )
    query_part = (query_part * (head_scale[None, :, None] / jnp.sqrt(jnp.float32(depth)))).astype(
        jnp.bfloat16
    )
    key_part = norm_keys(qkv[:, width : 2 * width], head_count)
    value_part = qkv[:, 2 * width :].astype(jnp.bfloat16)
    key_ext, value_ext = (
        padded_2(key_part, (("lat", 0),), alon),
        padded_2(value_part, (("lat", 0),), alon),
    )
    key_rows = key_ext.reshape(3 * alon, head_count, depth)
    global_rows = position * arows + 0 - 1 + jnp.arange(3 * alon, dtype=jnp.int32) // alon
    valid = (global_rows >= 0) & (global_rows < arows * band_count)
    pieces = attend(query_part, key_rows, value_ext, valid)
    after = start + jnp.dot(pieces, w_out, preferred_element_type=jnp.float32)
    atmos_next = after.astype(jnp.bfloat16)
    flux_in = rms_norm(after, gain_flux).astype(jnp.bfloat16)
    fluxes = jnp.einsum(
        "td,df->ft", flux_in, w_flux, preferred_element_type=jnp.float32
    ).astype(jnp.bfloat16)[None]
    flux_rows = jnp.concatenate(
        [shifted(fluxes, 2), shifted(fluxes, 1), fluxes, shifted(fluxes, -1), shifted(fluxes, -2)]
    )
    packed = jnp.concatenate(
        [ocean_state.transpose(1, 0, 2), land_mask.astype(jnp.bfloat16)[:, None, :]], axis=1
    )
    packed_low, packed_high = shifted(packed, 1), shifted(packed, -1)
    och = ocean_state.shape[0]
    state_parts = [packed_low[:, :och], packed[:, :och], packed_high[:, :och]]
    mask = jnp.concatenate([packed_low[:, och], packed[:, och], packed_high[:, och]])
    bands = jnp.concatenate([flux_start.astype(jnp.float32)[:, None], flux_weight], axis=1)
    bands = jnp.concatenate([shifted(bands, 1), bands, shifted(bands, -1)])
    flux_matrix = band_matrix(
        bands[:, 0].astype(jnp.int32), bands[:, 1:], position * arows - 2, arows + 4
    )
    ocean_next = ocean_steps(
        state_parts, mask, flux_rows, flux_matrix, conv_first, conv_second, position, band_count
    )
    return (atmos_next, ocean_next.transpose(1, 0, 2))


def solution(mesh):
    in_specs = (
        P(("ens", "lat"), None),
        P(None, ("ens", "lat"), None),
        P("lat", None),
        P(),
        P(),
        P(),
        P(),
        P(),
        P(),
        P(),
        P("lat"),
        P("lat", None),
        P("lat"),
        P("lat", None),
        P(),
        P(),
    )
    out_specs = (P(("ens", "lat"), None), P(None, ("ens", "lat"), None))
    return jax.shard_map(local, mesh=mesh, in_specs=in_specs, out_specs=out_specs, check_vma=False)
```

```python
import jax
import jax.numpy as jnp
from jax import lax
from jax.experimental import pallas as pl
from jax.experimental.pallas import tpu as pltpu
from jax.sharding import PartitionSpec as P

LEVELS = 19
VARS = 4
SPAN = 4
OSTEPS = 2


def rms_norm(values, scaling):
    return values * lax.rsqrt(jnp.mean(values * values, axis=-1, keepdims=True) + 1e-06) * scaling


def band_matrix(starts, weight, first_col, col_count):
    columns = first_col + jnp.arange(col_count, dtype=jnp.int32)
    summed = jnp.zeros((starts.shape[0], col_count), jnp.float32)
    for offset in range(weight.shape[1]):
        matches = (columns[None, :] == starts[:, None] + offset).astype(jnp.float32)
        summed = summed + weight[:, offset : offset + 1] * matches
    return summed


def atmos_kernel(surf_mat, flux_mat, scale_ref, atmos_ref, top_ref, mean_ref, embed_ref, gain_ref,
                 flux_gain_ref, qkv_ref, wout_ref, wflux_ref, ocean_ref,
                 after_ref, flux_mid, flux_low, flux_high, ocean_low, ocean_high,
                 surf, near, near_q, near_k, near_v, held, rows, send_sems, recv_sems):
    me = lax.axis_index("lat")
    count = lax.axis_size("lat")
    token_count, width = atmos_ref.shape
    group = near_q.shape[2]
    groups = width // group
    depth = width // scale_ref.shape[0]
    per_group = group // depth
    has = (me > 0, me < count - 1)
    target = (me - 1, me + 1)

    def send(kind, side, source, dest):
        return pltpu.make_async_remote_copy(
            src_ref=source,
            dst_ref=dest,
            send_sem=send_sems.at[kind, side],
            recv_sem=recv_sems.at[kind, side],
            device_id={"lat": target[side]},
            device_id_type=pl.DeviceIdType.MESH,
        )

    def start_both(kind, source, to_high, to_low):
        @pl.when(has[0])
        def _():
            send(kind, 0, source, to_high).start()

        @pl.when(has[1])
        def _():
            send(kind, 1, source, to_low).start()

    def wait_both(kind, source, to_high, to_low):
        @pl.when(has[0])
        def _():
            send(kind, 1, source, to_low).wait_recv()
            send(kind, 0, source, to_high).wait_send()

        @pl.when(has[1])
        def _():
            send(kind, 0, source, to_high).wait_recv()
            send(kind, 1, source, to_low).wait_send()

    barrier = pltpu.get_barrier_semaphore()
    for side in range(2):
        @pl.when(has[side])
        def _(side=side):
            pl.semaphore_signal(
                barrier, inc=1, device_id={"lat": target[side]},
                device_id_type=pl.DeviceIdType.MESH,
            )

    @pl.when(jnp.logical_not(has[0]))
    def _():
        surf[0] = jnp.zeros_like(surf[0])
        near[0] = jnp.zeros_like(near[0])
        rows[0] = jnp.zeros_like(rows[0])
        flux_low[...] = jnp.zeros_like(flux_low)

    @pl.when(jnp.logical_not(has[1]))
    def _():
        surf[2] = jnp.zeros_like(surf[2])
        near[2] = jnp.zeros_like(near[2])
        rows[2] = jnp.zeros_like(rows[2])
        flux_high[...] = jnp.zeros_like(flux_high)

    surf[1] = (
        jnp.dot(top_ref[...], mean_ref[...], preferred_element_type=jnp.float32) * (1.0 / SPAN)
    ).astype(jnp.bfloat16)
    pl.semaphore_wait(barrier, jnp.where(has[0], 1, 0) + jnp.where(has[1], 1, 0))
    surf_args = (0, surf.at[1], surf.at[2], surf.at[0])
    start_both(*surf_args)
    wait_both(*surf_args)
    band = jnp.zeros((VARS, surf.shape[2]), jnp.float32)
    for part in range(3):
        block = surf[part].astype(jnp.float32)
        for i in range(block.shape[0] // VARS):
            weight = surf_mat[0, part * (block.shape[0] // VARS) + i]
            band = band + weight * block[i * VARS : (i + 1) * VARS]
    band = jnp.concatenate([band, jnp.zeros_like(band)], axis=0)
    started = atmos_ref[...].astype(jnp.float32) + lax.dot_general(
        band, embed_ref[...], (((0,), (0,)), ((), ())), precision=lax.Precision.HIGHEST,
        preferred_element_type=jnp.float32,
    )
    held[...] = started
    near[1] = rms_norm(started, gain_ref[...]).astype(jnp.bfloat16)
    near_args = (1, near.at[1], near.at[2], near.at[0])
    ocean_args = (2, ocean_ref, ocean_high, ocean_low)
    start_both(*near_args)
    start_both(*ocean_args)

    lane = lax.broadcasted_iota(jnp.int32, (1, group), 1) // depth

    def head_scales(raw):
        squares = raw * raw
        factor = jnp.zeros_like(raw)
        for h in range(per_group):
            total = jnp.sum(jnp.where(lane == h, squares, 0.0), axis=1, keepdims=True)
            factor = jnp.where(lane == h, lax.rsqrt(total * (1.0 / depth) + 1e-06), factor)
        return raw * factor

    def project(part, column):
        return jnp.dot(
            near[part], qkv_ref[:, pl.ds(pl.multiple_of(column, group), group)],
            preferred_element_type=jnp.float32,
        )

    def own(g, carry):
        column = g * group
        query = head_scales(project(1, column))
        scale = jnp.zeros((1, group), jnp.float32)
        for h in range(per_group):
            scale = jnp.where(lane == h, scale_ref[g * per_group + h], scale)
        near_q[g] = (query * (scale * (1.0 / depth**0.5))).astype(jnp.bfloat16)
        near_k[g, 1] = head_scales(project(1, width + column)).astype(jnp.bfloat16)
        near_v[g, 1] = project(1, 2 * width + column).astype(jnp.bfloat16)
        return carry

    lax.fori_loop(0, groups, own, 0)
    wait_both(*near_args)

    def attend(g, carry):
        column = g * group
        for part in (0, 2):
            near_k[g, part] = head_scales(project(part, width + column)).astype(jnp.bfloat16)
            near_v[g, part] = project(part, 2 * width + column).astype(jnp.bfloat16)
        queries = near_q[g]
        mixed = jnp.zeros((token_count, group), jnp.float32)
        for h in range(per_group):
            query = jnp.where(lane == h, queries, jnp.zeros_like(queries))
            scores = []
            for part in range(3):
                score = lax.dot_general(
                    query, near_k[g, part], (((1,), (1,)), ((), ())),
                    preferred_element_type=jnp.float32,
                )
                if part != 1:
                    score = jnp.where(has[part // 2], score, -1e30)
                scores.append(score)
            largest = jnp.max(jnp.maximum(jnp.maximum(scores[0], scores[1]), scores[2]),
                              axis=1, keepdims=True)
            raised = [jnp.exp(score - largest) for score in scores]
            total = jnp.sum(raised[0] + raised[1] + raised[2], axis=1, keepdims=True)
            inverse = 1.0 / total
            value = jnp.zeros((token_count, group), jnp.float32)
            for part in range(3):
                value = value + jnp.dot(
                    (raised[part] * inverse).astype(jnp.bfloat16), near_v[g, part],
                    preferred_element_type=jnp.float32,
                )
            mixed = jnp.where(lane == h, value, mixed)
        held[...] += jnp.dot(
            mixed.astype(jnp.bfloat16), wout_ref[pl.ds(pl.multiple_of(column, group), group), :],
            preferred_element_type=jnp.float32,
        )
        return carry

    lax.fori_loop(0, groups, attend, 0)
    after = held[...]
    after_ref[...] = after.astype(jnp.bfloat16)
    flux_in = rms_norm(after, flux_gain_ref[...]).astype(jnp.bfloat16)
    rows[1] = lax.dot_general(
        wflux_ref[...], flux_in, (((1,), (1,)), ((), ())), preferred_element_type=jnp.float32
    ).astype(jnp.bfloat16)
    rows_args = (3, rows.at[1], rows.at[2], rows.at[0])
    start_both(*rows_args)
    wait_both(*rows_args)
    sources = [rows[part].astype(jnp.float32) for part in range(3)]
    for i in range(flux_mid.shape[0]):
        flux_mid[i] = (
            flux_mat[i, 0] * sources[0] + flux_mat[i, 1] * sources[1] + flux_mat[i, 2] * sources[2]
        ).astype(jnp.bfloat16)
    flux_args = (4, flux_mid, flux_high, flux_low)
    start_both(*flux_args)
    wait_both(*ocean_args)
    wait_both(*flux_args)


def atmos_block(surf_mat, flux_mat, head_scale, atmos, top, gain_attn, gain_flux, w_qkv, w_out,
                w_flux, surf_embed, packed):
    token_count, width = atmos.shape
    alon = top.shape[1] // SPAN
    orows = packed.shape[0]
    nflux = w_flux.shape[1]
    group = 256
    groups = width // group
    index = jnp.arange(top.shape[1], dtype=jnp.int32) // SPAN
    mean = (index[:, None] == jnp.arange(alon, dtype=jnp.int32)[None, :]).astype(jnp.bfloat16)
    embed = jnp.pad(surf_embed, ((0, VARS), (0, 0)))
    vmem = pl.BlockSpec(memory_space=pltpu.VMEM)
    smem = pl.BlockSpec(memory_space=pltpu.SMEM)
    anywhere = pl.BlockSpec(memory_space=pl.ANY)
    flux_shape = jax.ShapeDtypeStruct((orows, nflux, alon), jnp.bfloat16)
    ocean_shape = jax.ShapeDtypeStruct(packed.shape, packed.dtype)
    return pl.pallas_call(
        atmos_kernel,
        out_shape=[
            jax.ShapeDtypeStruct((token_count, width), jnp.bfloat16),
            flux_shape, flux_shape, flux_shape, ocean_shape, ocean_shape,
        ],
        in_specs=[smem] * 3 + [vmem] * 9 + [anywhere],
        out_specs=[vmem] * 4 + [anywhere] * 2,
        scratch_shapes=[
            pltpu.VMEM((3, top.shape[0], alon), jnp.bfloat16),
            pltpu.VMEM((3, token_count, width), jnp.bfloat16),
            pltpu.VMEM((groups, token_count, group), jnp.bfloat16),
            pltpu.VMEM((groups, 3, token_count, group), jnp.bfloat16),
            pltpu.VMEM((groups, 3, token_count, group), jnp.bfloat16),
            pltpu.VMEM((token_count, width), jnp.float32),
            pltpu.VMEM((3, nflux, alon), jnp.bfloat16),
            pltpu.SemaphoreType.DMA((5, 2)),
            pltpu.SemaphoreType.DMA((5, 2)),
        ],
        compiler_params=pltpu.CompilerParams(
            collective_id=0, has_side_effects=True, vmem_limit_bytes=58 * 1024 * 1024
        ),
        name="atmos_block",
    )(surf_mat, flux_mat, head_scale, atmos, top, mean, embed, gain_attn[None, :],
      gain_flux[None, :], w_qkv, w_out, w_flux.T, packed)


def ocean_kernel(pos_ref, low_ref, mid_ref, high_ref,
                 flux_low, flux_mid, flux_high, spread_ref,
                 first_ref, second_ref, out_ref, xs, hs, st, sea):
    och = mid_ref.shape[1] - 1
    olon = mid_ref.shape[2]
    orows = mid_ref.shape[0]
    wide = xs.shape[1]
    nflux = flux_mid.shape[1]
    hid = first_ref.shape[0] // 3
    opad = second_ref.shape[0] // 3
    stride = opad + nflux
    first_row = pos_ref[0]
    total = pos_ref[1]
    tail = wide - 128
    first_pad = olon - tail

    def wrap(head, last):
        lane = lax.broadcasted_iota(jnp.int32, last.shape, 1)
        end = pltpu.roll(last, 128 - first_pad, 1)
        begin = pltpu.roll(head, first_pad, 1)
        return jnp.where(lane == first_pad, begin, jnp.where(lane == 127, end, last))

    def combine(full, size):
        left = pltpu.roll(full[0:size], 1, 1)
        right = pltpu.roll(full[2 * size : 3 * size], wide - 1, 1)
        return left + full[size : 2 * size] + right

    sides = ((low_ref, flux_low), (mid_ref, flux_mid), (high_ref, flux_high))
    for part, (ref, flux) in enumerate(sides):
        def fill(i, carry, ref=ref, flux=flux, part=part):
            row = part * orows + i
            place = first_row + row - orows
            packed = ref[i].astype(jnp.float32)
            packed = jnp.where((place >= 0) & (place < total), packed, 0.0)
            state = packed[0:och]
            sea[row, :, 0:tail] = packed[och:, 0:tail]
            sea[row, :, tail:] = jnp.concatenate(
                [packed[och:, tail:], jnp.zeros((1, wide - olon), jnp.float32)], axis=1
            )
            state = jnp.concatenate([state, jnp.zeros((opad - och, olon), jnp.float32)], axis=0)
            last = jnp.concatenate(
                [state[:, tail:], jnp.zeros((opad, wide - olon), jnp.float32)], axis=1
            )
            st[row, :, 0:tail] = state[:, 0:tail]
            st[row, :, tail:] = wrap(state[:, 0:128], last)
            base = pl.multiple_of(row * stride, 16)
            xs[pl.ds(base, opad), :] = st[row].astype(jnp.bfloat16)
            spread = jnp.dot(flux[i], spread_ref[...], preferred_element_type=jnp.float32)
            base = pl.multiple_of(row * stride + opad, 16)
            xs[pl.ds(base, nflux), :] = spread.astype(jnp.bfloat16)
            return carry
        lax.fori_loop(0, orows, fill, 0)

    for step in range(OSTEPS):
        edge = 1 + 2 * step

        def first(row, carry):
            block = xs[pl.ds(pl.multiple_of((row - 1) * stride, 16), 3 * stride), :]
            full = jnp.dot(first_ref[...], block, preferred_element_type=jnp.float32)
            hidden = jax.nn.gelu(combine(full, hid), approximate=True)
            place = first_row + row - orows
            inside = jnp.where((place >= 0) & (place < total), 1.0, 0.0).astype(jnp.float32)
            hidden = hidden * inside
            base = pl.multiple_of(row * hid, 16)
            hs[pl.ds(base, hid), 0:tail] = hidden[:, 0:tail].astype(jnp.bfloat16)
            hs[pl.ds(base, hid), tail:] = wrap(hidden[:, 0:128], hidden[:, tail:]).astype(jnp.bfloat16)
            return carry
        lax.fori_loop(edge, 3 * orows - edge, first, 0)

        def second(row, carry):
            block = hs[pl.ds(pl.multiple_of((row - 1) * hid, 16), 3 * hid), :]
            full = jnp.dot(second_ref[...], block, preferred_element_type=jnp.float32)
            state = st[row] + sea[row] * combine(full, opad)
            if step == OSTEPS - 1:
                out_ref[row - orows] = state[0:och, 0:olon].astype(jnp.bfloat16)
            else:
                st[row, :, 0:tail] = state[:, 0:tail]
                st[row, :, tail:] = wrap(state[:, 0:128], state[:, tail:])
                base = pl.multiple_of(row * stride, 16)
                xs[pl.ds(base, opad), :] = st[row].astype(jnp.bfloat16)
            return carry
        lax.fori_loop(edge + 1, 3 * orows - edge - 1, second, 0)


def round_up(value, unit):
    return (value + unit - 1) // unit * unit


def ocean_steps(state_parts, fluxes, conv_first, conv_second, position, band_count):
    orows, _, olon = state_parts[1].shape
    och = conv_second.shape[1]
    nflux = fluxes[1].shape[1]
    hid = conv_first.shape[1]
    opad = round_up(och, 16)
    wide = round_up(olon + 2, 128)
    alon = fluxes[1].shape[2]
    first = conv_first.reshape(3, 3, hid, och + nflux)
    first = jnp.concatenate(
        [first[..., :och], jnp.zeros((3, 3, hid, opad - och), first.dtype), first[..., och:]], axis=3
    )
    first = first.transpose(1, 2, 0, 3).reshape(3 * hid, 3 * (opad + nflux))
    second = jnp.pad(conv_second.reshape(3, 3, och, hid), ((0, 0), (0, 0), (0, opad - och), (0, 0)))
    second = second.transpose(1, 2, 0, 3).reshape(3 * opad, 3 * hid)
    column = jnp.arange(wide, dtype=jnp.int32)
    longitude = jnp.where(column < olon, column, jnp.where(column == olon, 0, olon - 1))
    spread = (longitude[None, :] // SPAN == jnp.arange(alon, dtype=jnp.int32)[:, None]).astype(jnp.bfloat16)
    scalars = jnp.stack([position * orows, band_count * orows]).astype(jnp.int32)
    vmem = pl.BlockSpec(memory_space=pltpu.VMEM)
    smem = pl.BlockSpec(memory_space=pltpu.SMEM)
    return pl.pallas_call(
        ocean_kernel,
        out_shape=jax.ShapeDtypeStruct((orows, och, olon), jnp.bfloat16),
        in_specs=[smem] + [vmem] * 9,
        out_specs=vmem,
        scratch_shapes=[
            pltpu.VMEM((3 * orows * (opad + nflux), wide), jnp.bfloat16),
            pltpu.VMEM((3 * orows * hid, wide), jnp.bfloat16),
            pltpu.VMEM((3 * orows, opad, wide), jnp.float32),
            pltpu.VMEM((3 * orows, 1, wide), jnp.float32),
        ],
        compiler_params=pltpu.CompilerParams(vmem_limit_bytes=60 * 1024 * 1024),
        name="ocean_steps",
    )(scalars, *state_parts, *fluxes, spread, first, second)


def local(
    atmos,
    ocean_state,
    land_mask,
    w_qkv,
    w_out,
    head_scale,
    gain_attn,
    gain_flux,
    w_flux,
    surf_embed,
    flux_start,
    flux_weight,
    surf_start,
    surf_weight,
    conv_first,
    conv_second,
):
    position = lax.axis_index("lat")
    band_count = lax.axis_size("lat")
    orows = ocean_state.shape[1]
    packed = jnp.concatenate(
        [ocean_state.transpose(1, 0, 2), land_mask.astype(jnp.bfloat16)[:, None, :]], axis=1
    )
    top = ocean_state[::LEVELS].transpose(1, 0, 2).reshape(orows * VARS, -1)
    first_column = (position - 1) * orows
    surf_mat = band_matrix(surf_start, surf_weight, first_column, 3 * orows)
    columns = first_column + jnp.arange(3 * orows, dtype=jnp.int32)
    surf_mat = jnp.where((columns >= 0) & (columns < band_count * orows), surf_mat, 0.0)
    flux_mat = band_matrix(flux_start, flux_weight, position - 1, 3)
    atmos_next, flux_mid, flux_low, flux_high, ocean_low, ocean_high = atmos_block(
        surf_mat, flux_mat, head_scale, atmos, top, gain_attn, gain_flux, w_qkv, w_out, w_flux,
        surf_embed, packed,
    )
    ocean_next = ocean_steps(
        [ocean_low, packed, ocean_high], [flux_low, flux_mid, flux_high], conv_first, conv_second,
        position, band_count,
    )
    return (atmos_next, ocean_next.transpose(1, 0, 2))


def solution(mesh):
    in_specs = (
        P(("ens", "lat"), None),
        P(None, ("ens", "lat"), None),
        P("lat", None),
        P(),
        P(),
        P(),
        P(),
        P(),
        P(),
        P(),
        P("lat"),
        P("lat", None),
        P("lat"),
        P("lat", None),
        P(),
        P(),
    )
    out_specs = (P(("ens", "lat"), None), P(None, ("ens", "lat"), None))
    return jax.shard_map(local, mesh=mesh, in_specs=in_specs, out_specs=out_specs, check_vma=False)
```

```python
import jax
import jax.numpy as jnp
from jax import lax
from jax.experimental import pallas as pl
from jax.experimental.pallas import tpu as pltpu
from jax.sharding import PartitionSpec as P

LEVELS = 19
VARS = 4
SPAN = 4
OSTEPS = 2


def rms_norm(values, scaling):
    return values * lax.rsqrt(jnp.mean(values * values, axis=-1, keepdims=True) + 1e-06) * scaling


def atmos_kernel(surf_first, surf_weight, flux_first, flux_weight, scale_ref, atmos_ref, top_ref,
                 embed_ref, gain_ref, flux_gain_ref, qkv_ref, wout_ref, wflux_ref, ocean_ref,
                 land_ref,
                 after_ref, flux_mid, flux_low, flux_high, ocean_low, ocean_high, land_low, land_high,
                 surf, near, near_q, near_k, near_v, held, rows, send_sems, recv_sems):
    me = lax.axis_index("lat")
    count = lax.axis_size("lat")
    token_count, width = atmos_ref.shape
    group = near_q.shape[2]
    groups = width // group
    depth = width // scale_ref.shape[0]
    per_group = group // depth
    has = (me > 0, me < count - 1)
    target = (me - 1, me + 1)

    def send(kind, side, source, dest):
        return pltpu.make_async_remote_copy(
            src_ref=source,
            dst_ref=dest,
            send_sem=send_sems.at[kind, side],
            recv_sem=recv_sems.at[kind, side],
            device_id={"lat": target[side]},
            device_id_type=pl.DeviceIdType.MESH,
        )

    def start_both(kind, source, to_high, to_low):
        @pl.when(has[0])
        def _():
            send(kind, 0, source, to_high).start()

        @pl.when(has[1])
        def _():
            send(kind, 1, source, to_low).start()

    def wait_both(kind, source, to_high, to_low):
        @pl.when(has[0])
        def _():
            send(kind, 1, source, to_low).wait_recv()
            send(kind, 0, source, to_high).wait_send()

        @pl.when(has[1])
        def _():
            send(kind, 0, source, to_high).wait_recv()
            send(kind, 1, source, to_low).wait_send()

    barrier = pltpu.get_barrier_semaphore()
    for side in range(2):
        @pl.when(has[side])
        def _(side=side):
            pl.semaphore_signal(
                barrier, inc=1, device_id={"lat": target[side]},
                device_id_type=pl.DeviceIdType.MESH,
            )

    @pl.when(jnp.logical_not(has[0]))
    def _():
        surf[0] = jnp.zeros_like(surf[0])
        near[0] = jnp.zeros_like(near[0])
        rows[0] = jnp.zeros_like(rows[0])
        flux_low[...] = jnp.zeros_like(flux_low)

    @pl.when(jnp.logical_not(has[1]))
    def _():
        surf[2] = jnp.zeros_like(surf[2])
        near[2] = jnp.zeros_like(near[2])
        rows[2] = jnp.zeros_like(rows[2])
        flux_high[...] = jnp.zeros_like(flux_high)

    olon = top_ref.shape[1]
    alon = olon // SPAN
    spans = lax.broadcasted_iota(jnp.int32, (olon, alon), 0) // SPAN
    chosen = spans == lax.broadcasted_iota(jnp.int32, (olon, alon), 1)
    mean = jnp.where(chosen, 1.0, 0.0).astype(jnp.bfloat16)
    surf[1] = (
        jnp.dot(top_ref[...], mean, preferred_element_type=jnp.float32) * (1.0 / SPAN)
    ).astype(jnp.bfloat16)
    pl.semaphore_wait(barrier, jnp.where(has[0], 1, 0) + jnp.where(has[1], 1, 0))
    surf_args = (0, surf.at[1], surf.at[2], surf.at[0])
    start_both(*surf_args)
    wait_both(*surf_args)
    band = jnp.zeros((VARS, surf.shape[2]), jnp.float32)
    for part in range(3):
        block = surf[part].astype(jnp.float32)
        for i in range(block.shape[0] // VARS):
            rows_here = block.shape[0] // VARS
            column = (me + part - 1) * rows_here + i
            weight = jnp.float32(0.0)
            for b in range(surf_weight.shape[1]):
                weight = weight + jnp.where(surf_first[0] + b == column, surf_weight[0, b], 0.0)
            weight = jnp.where((column >= 0) & (column < count * rows_here), weight, 0.0)
            band = band + weight * block[i * VARS : (i + 1) * VARS]
    band = jnp.concatenate([band, jnp.zeros_like(band)], axis=0)
    embed = jnp.concatenate([embed_ref[...], jnp.zeros_like(embed_ref[...])], axis=0)
    started = atmos_ref[...].astype(jnp.float32) + lax.dot_general(
        band, embed, (((0,), (0,)), ((), ())), precision=lax.Precision.HIGHEST,
        preferred_element_type=jnp.float32,
    )
    held[...] = started
    near[1] = rms_norm(started, gain_ref[...]).astype(jnp.bfloat16)
    near_args = (1, near.at[1], near.at[2], near.at[0])
    ocean_args = (2, ocean_ref, ocean_high, ocean_low)
    land_args = (5, land_ref, land_high, land_low)
    start_both(*near_args)

    lane = lax.broadcasted_iota(jnp.int32, (1, group), 1) // depth

    def head_scales(raw):
        squares = raw * raw
        factor = jnp.zeros_like(raw)
        for h in range(per_group):
            total = jnp.sum(jnp.where(lane == h, squares, 0.0), axis=1, keepdims=True)
            factor = jnp.where(lane == h, lax.rsqrt(total * (1.0 / depth) + 1e-06), factor)
        return raw * factor

    def project(part, column):
        return jnp.dot(
            near[part], qkv_ref[:, pl.ds(pl.multiple_of(column, group), group)],
            preferred_element_type=jnp.float32,
        )

    def own(g, carry):
        column = g * group
        query = head_scales(project(1, column))
        scale = jnp.zeros((1, group), jnp.float32)
        for h in range(per_group):
            scale = jnp.where(lane == h, scale_ref[g * per_group + h], scale)
        near_q[g] = (query * (scale * (1.0 / depth**0.5))).astype(jnp.bfloat16)
        near_k[g, 1] = head_scales(project(1, width + column)).astype(jnp.bfloat16)
        near_v[g, 1] = project(1, 2 * width + column).astype(jnp.bfloat16)
        return carry

    lax.fori_loop(0, groups, own, 0)
    wait_both(*near_args)
    start_both(*ocean_args)
    start_both(*land_args)

    def attend(g, carry):
        column = g * group
        for part in (0, 2):
            near_k[g, part] = head_scales(project(part, width + column)).astype(jnp.bfloat16)
            near_v[g, part] = project(part, 2 * width + column).astype(jnp.bfloat16)
        queries = near_q[g]
        mixed = jnp.zeros((token_count, group), jnp.float32)
        for h in range(per_group):
            query = jnp.where(lane == h, queries, jnp.zeros_like(queries))
            scores = []
            for part in range(3):
                score = lax.dot_general(
                    query, near_k[g, part], (((1,), (1,)), ((), ())),
                    preferred_element_type=jnp.float32,
                )
                if part != 1:
                    score = jnp.where(has[part // 2], score, -1e30)
                scores.append(score)
            largest = jnp.max(jnp.maximum(jnp.maximum(scores[0], scores[1]), scores[2]),
                              axis=1, keepdims=True)
            raised = [jnp.exp(score - largest) for score in scores]
            total = jnp.sum(raised[0] + raised[1] + raised[2], axis=1, keepdims=True)
            inverse = 1.0 / total
            value = jnp.zeros((token_count, group), jnp.float32)
            for part in range(3):
                value = value + jnp.dot(
                    (raised[part] * inverse).astype(jnp.bfloat16), near_v[g, part],
                    preferred_element_type=jnp.float32,
                )
            mixed = jnp.where(lane == h, value, mixed)
        held[...] += jnp.dot(
            mixed.astype(jnp.bfloat16), wout_ref[pl.ds(pl.multiple_of(column, group), group), :],
            preferred_element_type=jnp.float32,
        )
        return carry

    lax.fori_loop(0, groups, attend, 0)
    after = held[...]
    after_ref[...] = after.astype(jnp.bfloat16)
    flux_in = rms_norm(after, flux_gain_ref[...]).astype(jnp.bfloat16)
    rows[1] = lax.dot_general(
        wflux_ref[...], flux_in, (((1,), (1,)), ((), ())), preferred_element_type=jnp.float32
    ).astype(jnp.bfloat16)
    rows_args = (3, rows.at[1], rows.at[2], rows.at[0])
    start_both(*rows_args)
    wait_both(*rows_args)
    sources = [rows[part].astype(jnp.float32) for part in range(3)]
    for i in range(flux_mid.shape[0]):
        regridded = jnp.zeros_like(sources[0])
        for part in range(3):
            weight = jnp.float32(0.0)
            for b in range(flux_weight.shape[1]):
                weight = weight + jnp.where(flux_first[i] + b == me + part - 1, flux_weight[i, b], 0.0)
            regridded = regridded + weight * sources[part]
        flux_mid[i] = regridded.astype(jnp.bfloat16)
    flux_args = (4, flux_mid, flux_high, flux_low)
    start_both(*flux_args)
    wait_both(*ocean_args)
    wait_both(*land_args)
    wait_both(*flux_args)


def atmos_block(surf_start, surf_weight, flux_start, flux_weight, head_scale, atmos, top, gain_attn,
                gain_flux, w_qkv, w_out, w_flux, surf_embed, ocean, land_mask):
    token_count, width = atmos.shape
    alon = top.shape[1] // SPAN
    orows = ocean.shape[0]
    nflux = w_flux.shape[1]
    group = 256
    groups = width // group
    vmem = pl.BlockSpec(memory_space=pltpu.VMEM)
    smem = pl.BlockSpec(memory_space=pltpu.SMEM)
    anywhere = pl.BlockSpec(memory_space=pl.ANY)
    flux_shape = jax.ShapeDtypeStruct((orows, nflux, alon), jnp.bfloat16)
    ocean_shape = jax.ShapeDtypeStruct(ocean.shape, ocean.dtype)
    land_shape = jax.ShapeDtypeStruct(land_mask.shape, land_mask.dtype)
    return pl.pallas_call(
        atmos_kernel,
        out_shape=[
            jax.ShapeDtypeStruct((token_count, width), jnp.bfloat16),
            flux_shape, flux_shape, flux_shape, ocean_shape, ocean_shape, land_shape, land_shape,
        ],
        in_specs=[smem] * 5 + [vmem] * 8 + [anywhere] * 2,
        out_specs=[vmem] * 4 + [anywhere] * 4,
        scratch_shapes=[
            pltpu.VMEM((3, top.shape[0], alon), jnp.bfloat16),
            pltpu.VMEM((3, token_count, width), jnp.bfloat16),
            pltpu.VMEM((groups, token_count, group), jnp.bfloat16),
            pltpu.VMEM((groups, 3, token_count, group), jnp.bfloat16),
            pltpu.VMEM((groups, 3, token_count, group), jnp.bfloat16),
            pltpu.VMEM((token_count, width), jnp.float32),
            pltpu.VMEM((3, nflux, alon), jnp.bfloat16),
            pltpu.SemaphoreType.DMA((6, 2)),
            pltpu.SemaphoreType.DMA((6, 2)),
        ],
        compiler_params=pltpu.CompilerParams(
            collective_id=0, has_side_effects=True, vmem_limit_bytes=58 * 1024 * 1024
        ),
        name="atmos_block",
    )(surf_start, surf_weight, flux_start, flux_weight, head_scale, atmos, top, surf_embed,
      gain_attn[None, :], gain_flux[None, :], w_qkv, w_out, w_flux.T, ocean, land_mask)


def ocean_kernel(low_ref, mid_ref, high_ref, land_low, land_mid, land_high,
                 flux_low, flux_mid, flux_high,
                 first_ref, second_ref, out_ref, xs, hs, st, sea):
    och = mid_ref.shape[1]
    olon = mid_ref.shape[2]
    orows = mid_ref.shape[0]
    wide = xs.shape[1]
    nflux = flux_mid.shape[1]
    hid = first_ref.shape[0] // 3
    opad = second_ref.shape[0] // 3
    stride = opad + nflux
    first_row = lax.axis_index("lat") * orows
    total = lax.axis_size("lat") * orows
    alon = flux_mid.shape[2]
    column = lax.broadcasted_iota(jnp.int32, (alon, wide), 1)
    longitude = jnp.where(column < olon, column, jnp.where(column == olon, 0, olon - 1))
    chosen = longitude // SPAN == lax.broadcasted_iota(jnp.int32, (alon, wide), 0)
    repeat = jnp.where(chosen, 1.0, 0.0).astype(jnp.bfloat16)
    tail = wide - 128
    first_pad = olon - tail

    def wrap(head, last):
        lane = lax.broadcasted_iota(jnp.int32, last.shape, 1)
        end = pltpu.roll(last, 128 - first_pad, 1)
        begin = pltpu.roll(head, first_pad, 1)
        return jnp.where(lane == first_pad, begin, jnp.where(lane == 127, end, last))

    def combine(full, size):
        left = pltpu.roll(full[0:size], 1, 1)
        right = pltpu.roll(full[2 * size : 3 * size], wide - 1, 1)
        return left + full[size : 2 * size] + right

    sides = (
        (low_ref, land_low, flux_low), (mid_ref, land_mid, flux_mid), (high_ref, land_high, flux_high)
    )
    for part, (ref, land, flux) in enumerate(sides):
        def fill(i, carry, ref=ref, land=land, flux=flux, part=part):
            row = part * orows + i
            place = first_row + row - orows
            inside = (place >= 0) & (place < total)
            state = jnp.where(inside, ref[i].astype(jnp.float32), 0.0)
            cells = jnp.where(inside, land[pl.ds(i, 1), :].astype(jnp.float32), 0.0)
            sea[row, :, 0:tail] = cells[:, 0:tail]
            sea[row, :, tail:] = jnp.concatenate(
                [cells[:, tail:], jnp.zeros((1, wide - olon), jnp.float32)], axis=1
            )
            state = jnp.concatenate([state, jnp.zeros((opad - och, olon), jnp.float32)], axis=0)
            last = jnp.concatenate(
                [state[:, tail:], jnp.zeros((opad, wide - olon), jnp.float32)], axis=1
            )
            st[row, :, 0:tail] = state[:, 0:tail]
            st[row, :, tail:] = wrap(state[:, 0:128], last)
            base = pl.multiple_of(row * stride, 16)
            xs[pl.ds(base, opad), :] = st[row].astype(jnp.bfloat16)
            spread = jnp.dot(flux[i], repeat, preferred_element_type=jnp.float32)
            base = pl.multiple_of(row * stride + opad, 16)
            xs[pl.ds(base, nflux), :] = spread.astype(jnp.bfloat16)
            return carry
        lax.fori_loop(0, orows, fill, 0)

    for step in range(OSTEPS):
        edge = 1 + 2 * step

        def first(row, carry):
            block = xs[pl.ds(pl.multiple_of((row - 1) * stride, 16), 3 * stride), :]
            full = jnp.dot(first_ref[...], block, preferred_element_type=jnp.float32)
            hidden = jax.nn.gelu(combine(full, hid), approximate=True)
            place = first_row + row - orows
            inside = jnp.where((place >= 0) & (place < total), 1.0, 0.0).astype(jnp.float32)
            hidden = hidden * inside
            base = pl.multiple_of(row * hid, 16)
            hs[pl.ds(base, hid), 0:tail] = hidden[:, 0:tail].astype(jnp.bfloat16)
            hs[pl.ds(base, hid), tail:] = wrap(hidden[:, 0:128], hidden[:, tail:]).astype(jnp.bfloat16)
            return carry
        lax.fori_loop(edge, 3 * orows - edge, first, 0, unroll=2)

        def second(row, carry):
            block = hs[pl.ds(pl.multiple_of((row - 1) * hid, 16), 3 * hid), :]
            full = jnp.dot(second_ref[...], block, preferred_element_type=jnp.float32)
            state = st[row] + sea[row] * combine(full, opad)
            if step == OSTEPS - 1:
                out_ref[row - orows] = state[0:och, 0:olon].astype(jnp.bfloat16)
            else:
                st[row, :, 0:tail] = state[:, 0:tail]
                st[row, :, tail:] = wrap(state[:, 0:128], state[:, tail:])
                base = pl.multiple_of(row * stride, 16)
                xs[pl.ds(base, opad), :] = st[row].astype(jnp.bfloat16)
            return carry
        lax.fori_loop(edge + 1, 3 * orows - edge - 1, second, 0, unroll=2)


def round_up(value, unit):
    return (value + unit - 1) // unit * unit


def ocean_steps(state_parts, land_parts, fluxes, conv_first, conv_second):
    orows, _, olon = state_parts[1].shape
    och = conv_second.shape[1]
    nflux = fluxes[1].shape[1]
    hid = conv_first.shape[1]
    opad = round_up(och, 16)
    wide = round_up(olon + 2, 128)
    first = conv_first.reshape(3, 3, hid, och + nflux)
    first = jnp.concatenate(
        [first[..., :och], jnp.zeros((3, 3, hid, opad - och), first.dtype), first[..., och:]], axis=3
    )
    first = first.transpose(1, 2, 0, 3).reshape(3 * hid, 3 * (opad + nflux))
    second = jnp.pad(conv_second.reshape(3, 3, och, hid), ((0, 0), (0, 0), (0, opad - och), (0, 0)))
    second = second.transpose(1, 2, 0, 3).reshape(3 * opad, 3 * hid)
    vmem = pl.BlockSpec(memory_space=pltpu.VMEM)
    return pl.pallas_call(
        ocean_kernel,
        out_shape=jax.ShapeDtypeStruct((orows, och, olon), jnp.bfloat16),
        in_specs=[vmem] * 11,
        out_specs=vmem,
        scratch_shapes=[
            pltpu.VMEM((3 * orows * (opad + nflux), wide), jnp.bfloat16),
            pltpu.VMEM((3 * orows * hid, wide), jnp.bfloat16),
            pltpu.VMEM((3 * orows, opad, wide), jnp.float32),
            pltpu.VMEM((3 * orows, 1, wide), jnp.float32),
        ],
        compiler_params=pltpu.CompilerParams(vmem_limit_bytes=60 * 1024 * 1024),
        name="ocean_steps",
    )(*state_parts, *land_parts, *fluxes, first, second)


def local(
    atmos,
    ocean_state,
    land_mask,
    w_qkv,
    w_out,
    head_scale,
    gain_attn,
    gain_flux,
    w_flux,
    surf_embed,
    flux_start,
    flux_weight,
    surf_start,
    surf_weight,
    conv_first,
    conv_second,
):
    orows = ocean_state.shape[1]
    ocean = ocean_state.transpose(1, 0, 2)
    top = ocean_state[::LEVELS].transpose(1, 0, 2).reshape(orows * VARS, -1)
    outs = atmos_block(
        surf_start, surf_weight, flux_start, flux_weight, head_scale, atmos, top, gain_attn,
        gain_flux, w_qkv, w_out, w_flux, surf_embed, ocean, land_mask,
    )
    atmos_next, flux_mid, flux_low, flux_high, ocean_low, ocean_high, land_low, land_high = outs
    ocean_next = ocean_steps(
        [ocean_low, ocean, ocean_high], [land_low, land_mask, land_high],
        [flux_low, flux_mid, flux_high], conv_first, conv_second,
    )
    return (atmos_next, ocean_next.transpose(1, 0, 2))


def solution(mesh):
    in_specs = (
        P(("ens", "lat"), None),
        P(None, ("ens", "lat"), None),
        P("lat", None),
        P(),
        P(),
        P(),
        P(),
        P(),
        P(),
        P(),
        P("lat"),
        P("lat", None),
        P("lat"),
        P("lat", None),
        P(),
        P(),
    )
    out_specs = (P(("ens", "lat"), None), P(None, ("ens", "lat"), None))
    return jax.shard_map(local, mesh=mesh, in_specs=in_specs, out_specs=out_specs, check_vma=False)
```

```python
import jax
import jax.numpy as jnp
from jax import lax
from jax.experimental import pallas as pl
from jax.experimental.pallas import tpu as pltpu
from jax.sharding import PartitionSpec as P

LEVELS = 19
VARS = 4
SPAN = 4
OSTEPS = 2


def rms_norm(values, scaling):
    return values * lax.rsqrt(jnp.mean(values * values, axis=-1, keepdims=True) + 1e-06) * scaling


def atmos_kernel(surf_first, surf_weight, flux_first, flux_weight, scale_ref, atmos_ref, top_ref,
                 embed_ref, gain_ref, flux_gain_ref, qkv_ref, wout_ref, wflux_ref, ocean_ref,
                 land_ref,
                 after_ref, flux_mid, flux_low, flux_high, ocean_low, ocean_high, land_low, land_high,
                 surf, near, near_q, near_k, near_v, own_mixed, own_largest, own_total, held, rows,
                 qkv_here, wout_here, load_sems, send_sems, recv_sems):
    me = lax.axis_index("lat")
    count = lax.axis_size("lat")
    token_count, width = atmos_ref.shape
    group = near_q.shape[2]
    groups = width // group
    depth = width // scale_ref.shape[0]
    per_group = group // depth
    has = (me > 0, me < count - 1)
    target = (me - 1, me + 1)

    def send(kind, side, source, dest):
        return pltpu.make_async_remote_copy(
            src_ref=source,
            dst_ref=dest,
            send_sem=send_sems.at[kind, side],
            recv_sem=recv_sems.at[kind, side],
            device_id={"lat": target[side]},
            device_id_type=pl.DeviceIdType.MESH,
        )

    def start_both(kind, source, to_high, to_low):
        @pl.when(has[0])
        def _():
            send(kind, 0, source, to_high).start()

        @pl.when(has[1])
        def _():
            send(kind, 1, source, to_low).start()

    def wait_both(kind, source, to_high, to_low):
        @pl.when(has[0])
        def _():
            send(kind, 1, source, to_low).wait_recv()
            send(kind, 0, source, to_high).wait_send()

        @pl.when(has[1])
        def _():
            send(kind, 0, source, to_high).wait_recv()
            send(kind, 1, source, to_low).wait_send()

    loads = (
        pltpu.make_async_copy(qkv_ref, qkv_here, load_sems.at[0]),
        pltpu.make_async_copy(wout_ref, wout_here, load_sems.at[1]),
    )
    for load in loads:
        load.start()
    barrier = pltpu.get_barrier_semaphore()
    for side in range(2):
        @pl.when(has[side])
        def _(side=side):
            pl.semaphore_signal(
                barrier, inc=1, device_id={"lat": target[side]},
                device_id_type=pl.DeviceIdType.MESH,
            )

    @pl.when(jnp.logical_not(has[0]))
    def _():
        surf[0] = jnp.zeros_like(surf[0])
        near[0] = jnp.zeros_like(near[0])
        rows[0] = jnp.zeros_like(rows[0])
        flux_low[...] = jnp.zeros_like(flux_low)

    @pl.when(jnp.logical_not(has[1]))
    def _():
        surf[2] = jnp.zeros_like(surf[2])
        near[2] = jnp.zeros_like(near[2])
        rows[2] = jnp.zeros_like(rows[2])
        flux_high[...] = jnp.zeros_like(flux_high)

    olon = top_ref.shape[1]
    alon = olon // SPAN
    spans = lax.broadcasted_iota(jnp.int32, (olon, alon), 0) // SPAN
    chosen = spans == lax.broadcasted_iota(jnp.int32, (olon, alon), 1)
    mean = jnp.where(chosen, 1.0, 0.0).astype(jnp.bfloat16)
    surf[1] = (
        jnp.dot(top_ref[...], mean, preferred_element_type=jnp.float32) * (1.0 / SPAN)
    ).astype(jnp.bfloat16)
    pl.semaphore_wait(barrier, jnp.where(has[0], 1, 0) + jnp.where(has[1], 1, 0))
    surf_args = (0, surf.at[1], surf.at[2], surf.at[0])
    start_both(*surf_args)
    wait_both(*surf_args)
    band = jnp.zeros((VARS, surf.shape[2]), jnp.float32)
    for part in range(3):
        block = surf[part].astype(jnp.float32)
        for i in range(block.shape[0] // VARS):
            rows_here = block.shape[0] // VARS
            column = (me + part - 1) * rows_here + i
            weight = jnp.float32(0.0)
            for b in range(surf_weight.shape[1]):
                weight = weight + jnp.where(surf_first[0] + b == column, surf_weight[0, b], 0.0)
            weight = jnp.where((column >= 0) & (column < count * rows_here), weight, 0.0)
            band = band + weight * block[i * VARS : (i + 1) * VARS]
    band = jnp.concatenate([band, jnp.zeros_like(band)], axis=0)
    embed = jnp.concatenate([embed_ref[...], jnp.zeros_like(embed_ref[...])], axis=0)
    started = atmos_ref[...].astype(jnp.float32) + lax.dot_general(
        band, embed, (((0,), (0,)), ((), ())), precision=lax.Precision.HIGHEST,
        preferred_element_type=jnp.float32,
    )
    held[...] = started
    near[1] = rms_norm(started, gain_ref[...]).astype(jnp.bfloat16)
    near_args = (1, near.at[1], near.at[2], near.at[0])
    ocean_args = (2, ocean_ref, ocean_high, ocean_low)
    land_args = (5, land_ref, land_high, land_low)
    start_both(*near_args)

    lane = lax.broadcasted_iota(jnp.int32, (1, group), 1) // depth

    def head_scales(raw):
        squares = raw * raw
        factor = jnp.zeros_like(raw)
        for h in range(per_group):
            total = jnp.sum(jnp.where(lane == h, squares, 0.0), axis=1, keepdims=True)
            factor = jnp.where(lane == h, lax.rsqrt(total * (1.0 / depth) + 1e-06), factor)
        return raw * factor

    def project(part, column):
        return jnp.dot(
            near[part], qkv_here[:, pl.ds(pl.multiple_of(column, group), group)],
            preferred_element_type=jnp.float32,
        )

    def head_scores(queries, h, keys):
        query = jnp.where(lane == h, queries, jnp.zeros_like(queries))
        return lax.dot_general(
            query, keys, (((1,), (1,)), ((), ())), preferred_element_type=jnp.float32
        )

    def own(g, carry):
        column = g * group
        query = head_scales(project(1, column))
        scale = jnp.zeros((1, group), jnp.float32)
        for h in range(per_group):
            scale = jnp.where(lane == h, scale_ref[g * per_group + h], scale)
        near_q[g] = (query * (scale * (1.0 / depth**0.5))).astype(jnp.bfloat16)
        near_k[g, 1] = head_scales(project(1, width + column)).astype(jnp.bfloat16)
        near_v[g, 1] = project(1, 2 * width + column).astype(jnp.bfloat16)
        queries = near_q[g]
        mixed = jnp.zeros((token_count, group), jnp.float32)
        for h in range(per_group):
            score = head_scores(queries, h, near_k[g, 1])
            largest = jnp.max(score, axis=1, keepdims=True)
            raised = jnp.exp(score - largest)
            own_largest[g * per_group + h] = largest
            own_total[g * per_group + h] = jnp.sum(raised, axis=1, keepdims=True)
            value = jnp.dot(
                raised.astype(jnp.bfloat16), near_v[g, 1], preferred_element_type=jnp.float32
            )
            mixed = jnp.where(lane == h, value, mixed)
        own_mixed[g] = mixed
        return carry

    loads[0].wait()
    lax.fori_loop(0, groups, own, 0)
    loads[1].wait()
    wait_both(*near_args)
    start_both(*ocean_args)
    start_both(*land_args)

    def attend(g, carry):
        column = g * group
        for part in (0, 2):
            near_k[g, part] = head_scales(project(part, width + column)).astype(jnp.bfloat16)
            near_v[g, part] = project(part, 2 * width + column).astype(jnp.bfloat16)
        queries = near_q[g]
        mixed = jnp.zeros((token_count, group), jnp.float32)
        for h in range(per_group):
            low = jnp.where(has[0], head_scores(queries, h, near_k[g, 0]), -1e30)
            high = jnp.where(has[1], head_scores(queries, h, near_k[g, 2]), -1e30)
            before = own_largest[g * per_group + h]
            largest = jnp.maximum(
                jnp.max(jnp.maximum(low, high), axis=1, keepdims=True), before
            )
            low = jnp.exp(low - largest)
            high = jnp.exp(high - largest)
            fade = jnp.exp(before - largest)
            total = own_total[g * per_group + h] * fade + jnp.sum(low + high, axis=1, keepdims=True)
            value = jnp.dot(
                low.astype(jnp.bfloat16), near_v[g, 0], preferred_element_type=jnp.float32
            ) + jnp.dot(
                high.astype(jnp.bfloat16), near_v[g, 2], preferred_element_type=jnp.float32
            )
            value = (own_mixed[g] * fade + value) * (1.0 / total)
            mixed = jnp.where(lane == h, value, mixed)
        held[...] += jnp.dot(
            mixed.astype(jnp.bfloat16), wout_here[pl.ds(pl.multiple_of(column, group), group), :],
            preferred_element_type=jnp.float32,
        )
        return carry

    lax.fori_loop(0, groups, attend, 0)
    after = held[...]
    after_ref[...] = after.astype(jnp.bfloat16)
    flux_in = rms_norm(after, flux_gain_ref[...]).astype(jnp.bfloat16)
    rows[1] = lax.dot_general(
        wflux_ref[...], flux_in, (((1,), (1,)), ((), ())), preferred_element_type=jnp.float32
    ).astype(jnp.bfloat16)
    rows_args = (3, rows.at[1], rows.at[2], rows.at[0])
    start_both(*rows_args)
    wait_both(*rows_args)
    sources = [rows[part].astype(jnp.float32) for part in range(3)]
    for i in range(flux_mid.shape[0]):
        regridded = jnp.zeros_like(sources[0])
        for part in range(3):
            weight = jnp.float32(0.0)
            for b in range(flux_weight.shape[1]):
                weight = weight + jnp.where(flux_first[i] + b == me + part - 1, flux_weight[i, b], 0.0)
            regridded = regridded + weight * sources[part]
        flux_mid[i] = regridded.astype(jnp.bfloat16)
    flux_args = (4, flux_mid, flux_high, flux_low)
    start_both(*flux_args)
    wait_both(*ocean_args)
    wait_both(*land_args)
    wait_both(*flux_args)


def atmos_block(surf_start, surf_weight, flux_start, flux_weight, head_scale, atmos, top, gain_attn,
                gain_flux, w_qkv, w_out, w_flux, surf_embed, ocean, land_mask):
    token_count, width = atmos.shape
    alon = top.shape[1] // SPAN
    orows = ocean.shape[0]
    nflux = w_flux.shape[1]
    group = 256
    groups = width // group
    vmem = pl.BlockSpec(memory_space=pltpu.VMEM)
    smem = pl.BlockSpec(memory_space=pltpu.SMEM)
    anywhere = pl.BlockSpec(memory_space=pl.ANY)
    flux_shape = jax.ShapeDtypeStruct((orows, nflux, alon), jnp.bfloat16)
    ocean_shape = jax.ShapeDtypeStruct(ocean.shape, ocean.dtype)
    land_shape = jax.ShapeDtypeStruct(land_mask.shape, land_mask.dtype)
    return pl.pallas_call(
        atmos_kernel,
        out_shape=[
            jax.ShapeDtypeStruct((token_count, width), jnp.bfloat16),
            flux_shape, flux_shape, flux_shape, ocean_shape, ocean_shape, land_shape, land_shape,
        ],
        in_specs=[smem] * 5 + [vmem] * 5 + [anywhere] * 2 + [vmem] + [anywhere] * 2,
        out_specs=[vmem] * 4 + [anywhere] * 4,
        scratch_shapes=[
            pltpu.VMEM((3, top.shape[0], alon), jnp.bfloat16),
            pltpu.VMEM((3, token_count, width), jnp.bfloat16),
            pltpu.VMEM((groups, token_count, group), jnp.bfloat16),
            pltpu.VMEM((groups, 3, token_count, group), jnp.bfloat16),
            pltpu.VMEM((groups, 3, token_count, group), jnp.bfloat16),
            pltpu.VMEM((groups, token_count, group), jnp.float32),
            pltpu.VMEM((head_scale.shape[0], token_count, 1), jnp.float32),
            pltpu.VMEM((head_scale.shape[0], token_count, 1), jnp.float32),
            pltpu.VMEM((token_count, width), jnp.float32),
            pltpu.VMEM((3, nflux, alon), jnp.bfloat16),
            pltpu.VMEM(w_qkv.shape, w_qkv.dtype),
            pltpu.VMEM(w_out.shape, w_out.dtype),
            pltpu.SemaphoreType.DMA((2,)),
            pltpu.SemaphoreType.DMA((6, 2)),
            pltpu.SemaphoreType.DMA((6, 2)),
        ],
        compiler_params=pltpu.CompilerParams(
            collective_id=0, has_side_effects=True, vmem_limit_bytes=58 * 1024 * 1024
        ),
        name="atmos_block",
    )(surf_start, surf_weight, flux_start, flux_weight, head_scale, atmos, top, surf_embed,
      gain_attn[None, :], gain_flux[None, :], w_qkv, w_out, w_flux.T, ocean, land_mask)


def ocean_kernel(low_ref, mid_ref, high_ref, land_low, land_mid, land_high,
                 flux_low, flux_mid, flux_high,
                 first_ref, second_ref, out_ref, xs, hs, st, sea):
    och = mid_ref.shape[1]
    olon = mid_ref.shape[2]
    orows = mid_ref.shape[0]
    wide = xs.shape[1]
    nflux = flux_mid.shape[1]
    hid = first_ref.shape[0] // 3
    opad = second_ref.shape[0] // 3
    stride = opad + nflux
    first_row = lax.axis_index("lat") * orows
    total = lax.axis_size("lat") * orows
    alon = flux_mid.shape[2]
    column = lax.broadcasted_iota(jnp.int32, (alon, wide), 1)
    longitude = jnp.where(column < olon, column, jnp.where(column == olon, 0, olon - 1))
    chosen = longitude // SPAN == lax.broadcasted_iota(jnp.int32, (alon, wide), 0)
    repeat = jnp.where(chosen, 1.0, 0.0).astype(jnp.bfloat16)
    tail = wide - 128
    first_pad = olon - tail

    def wrap(head, last):
        lane = lax.broadcasted_iota(jnp.int32, last.shape, 1)
        end = pltpu.roll(last, 128 - first_pad, 1)
        begin = pltpu.roll(head, first_pad, 1)
        return jnp.where(lane == first_pad, begin, jnp.where(lane == 127, end, last))

    def combine(full, size):
        left = pltpu.roll(full[0:size], 1, 1)
        right = pltpu.roll(full[2 * size : 3 * size], wide - 1, 1)
        return left + full[size : 2 * size] + right

    sides = (
        (low_ref, land_low, flux_low), (mid_ref, land_mid, flux_mid), (high_ref, land_high, flux_high)
    )
    for part, (ref, land, flux) in enumerate(sides):
        def fill(i, carry, ref=ref, land=land, flux=flux, part=part):
            row = part * orows + i
            place = first_row + row - orows
            inside = (place >= 0) & (place < total)
            state = jnp.where(inside, ref[i].astype(jnp.float32), 0.0)
            cells = jnp.where(inside, land[pl.ds(i, 1), :].astype(jnp.float32), 0.0)
            sea[row, :, 0:tail] = cells[:, 0:tail]
            sea[row, :, tail:] = jnp.concatenate(
                [cells[:, tail:], jnp.zeros((1, wide - olon), jnp.float32)], axis=1
            )
            state = jnp.concatenate([state, jnp.zeros((opad - och, olon), jnp.float32)], axis=0)
            last = jnp.concatenate(
                [state[:, tail:], jnp.zeros((opad, wide - olon), jnp.float32)], axis=1
            )
            st[row, :, 0:tail] = state[:, 0:tail]
            st[row, :, tail:] = wrap(state[:, 0:128], last)
            base = pl.multiple_of(row * stride, 16)
            xs[pl.ds(base, opad), :] = st[row].astype(jnp.bfloat16)
            spread = jnp.dot(flux[i], repeat, preferred_element_type=jnp.float32)
            base = pl.multiple_of(row * stride + opad, 16)
            xs[pl.ds(base, nflux), :] = spread.astype(jnp.bfloat16)
            return carry
        lax.fori_loop(0, orows, fill, 0)

    for step in range(OSTEPS):
        edge = 1 + 2 * step

        def first(row, carry):
            block = xs[pl.ds(pl.multiple_of((row - 1) * stride, 16), 3 * stride), :]
            full = jnp.dot(first_ref[...], block, preferred_element_type=jnp.float32)
            hidden = jax.nn.gelu(combine(full, hid), approximate=True)
            place = first_row + row - orows
            inside = jnp.where((place >= 0) & (place < total), 1.0, 0.0).astype(jnp.float32)
            hidden = hidden * inside
            base = pl.multiple_of(row * hid, 16)
            hs[pl.ds(base, hid), 0:tail] = hidden[:, 0:tail].astype(jnp.bfloat16)
            hs[pl.ds(base, hid), tail:] = wrap(hidden[:, 0:128], hidden[:, tail:]).astype(jnp.bfloat16)
            return carry
        lax.fori_loop(edge, 3 * orows - edge, first, 0, unroll=2)

        def second(row, carry):
            block = hs[pl.ds(pl.multiple_of((row - 1) * hid, 16), 3 * hid), :]
            full = jnp.dot(second_ref[...], block, preferred_element_type=jnp.float32)
            state = st[row] + sea[row] * combine(full, opad)
            if step == OSTEPS - 1:
                out_ref[row - orows] = state[0:och, 0:olon].astype(jnp.bfloat16)
            else:
                st[row, :, 0:tail] = state[:, 0:tail]
                st[row, :, tail:] = wrap(state[:, 0:128], state[:, tail:])
                base = pl.multiple_of(row * stride, 16)
                xs[pl.ds(base, opad), :] = st[row].astype(jnp.bfloat16)
            return carry
        lax.fori_loop(edge + 1, 3 * orows - edge - 1, second, 0, unroll=2)


def round_up(value, unit):
    return (value + unit - 1) // unit * unit


def ocean_steps(state_parts, land_parts, fluxes, conv_first, conv_second):
    orows, _, olon = state_parts[1].shape
    och = conv_second.shape[1]
    nflux = fluxes[1].shape[1]
    hid = conv_first.shape[1]
    opad = round_up(och, 16)
    wide = round_up(olon + 2, 128)
    first = conv_first.reshape(3, 3, hid, och + nflux)
    first = jnp.concatenate(
        [first[..., :och], jnp.zeros((3, 3, hid, opad - och), first.dtype), first[..., och:]], axis=3
    )
    first = first.transpose(1, 2, 0, 3).reshape(3 * hid, 3 * (opad + nflux))
    second = jnp.pad(conv_second.reshape(3, 3, och, hid), ((0, 0), (0, 0), (0, opad - och), (0, 0)))
    second = second.transpose(1, 2, 0, 3).reshape(3 * opad, 3 * hid)
    vmem = pl.BlockSpec(memory_space=pltpu.VMEM)
    return pl.pallas_call(
        ocean_kernel,
        out_shape=jax.ShapeDtypeStruct((orows, och, olon), jnp.bfloat16),
        in_specs=[vmem] * 11,
        out_specs=vmem,
        scratch_shapes=[
            pltpu.VMEM((3 * orows * (opad + nflux), wide), jnp.bfloat16),
            pltpu.VMEM((3 * orows * hid, wide), jnp.bfloat16),
            pltpu.VMEM((3 * orows, opad, wide), jnp.float32),
            pltpu.VMEM((3 * orows, 1, wide), jnp.float32),
        ],
        compiler_params=pltpu.CompilerParams(vmem_limit_bytes=60 * 1024 * 1024),
        name="ocean_steps",
    )(*state_parts, *land_parts, *fluxes, first, second)


def local(
    atmos,
    ocean_state,
    land_mask,
    w_qkv,
    w_out,
    head_scale,
    gain_attn,
    gain_flux,
    w_flux,
    surf_embed,
    flux_start,
    flux_weight,
    surf_start,
    surf_weight,
    conv_first,
    conv_second,
):
    orows = ocean_state.shape[1]
    ocean = ocean_state.transpose(1, 0, 2)
    top = ocean_state[::LEVELS].transpose(1, 0, 2).reshape(orows * VARS, -1)
    outs = atmos_block(
        surf_start, surf_weight, flux_start, flux_weight, head_scale, atmos, top, gain_attn,
        gain_flux, w_qkv, w_out, w_flux, surf_embed, ocean, land_mask,
    )
    atmos_next, flux_mid, flux_low, flux_high, ocean_low, ocean_high, land_low, land_high = outs
    ocean_next = ocean_steps(
        [ocean_low, ocean, ocean_high], [land_low, land_mask, land_high],
        [flux_low, flux_mid, flux_high], conv_first, conv_second,
    )
    return (atmos_next, ocean_next.transpose(1, 0, 2))


def solution(mesh):
    in_specs = (
        P(("ens", "lat"), None),
        P(None, ("ens", "lat"), None),
        P("lat", None),
        P(),
        P(),
        P(),
        P(),
        P(),
        P(),
        P(),
        P("lat"),
        P("lat", None),
        P("lat"),
        P("lat", None),
        P(),
        P(),
    )
    out_specs = (P(("ens", "lat"), None), P(None, ("ens", "lat"), None))
    return jax.shard_map(local, mesh=mesh, in_specs=in_specs, out_specs=out_specs, check_vma=False)
```

```python
import jax
import jax.numpy as jnp
from jax import lax
from jax.experimental import pallas as pl
from jax.experimental.pallas import tpu as pltpu
from jax.sharding import PartitionSpec as P

LEVELS = 19
VARS = 4
SPAN = 4
OSTEPS = 2


def rms_norm(values, scaling):
    return values * lax.rsqrt(jnp.mean(values * values, axis=-1, keepdims=True) + 1e-06) * scaling


def atmos_kernel(surf_first, surf_weight, flux_first, flux_weight, scale_ref, atmos_ref, top_ref,
                 embed_ref, gain_ref, flux_gain_ref, qkv_ref, wout_ref, wflux_ref, ocean_ref,
                 land_ref,
                 after_ref, flux_mid, flux_low, flux_high, ocean_low, ocean_high, land_low, land_high,
                 surf, near, near_q, near_k, near_v, own_mixed, own_largest, own_total, held, rows,
                 qkv_here, wout_here, load_sems, send_sems, recv_sems):
    me = lax.axis_index("lat")
    count = lax.axis_size("lat")
    token_count, width = atmos_ref.shape
    group = near_q.shape[2]
    groups = width // group
    depth = width // scale_ref.shape[0]
    per_group = group // depth
    has = (me > 0, me < count - 1)
    target = (me - 1, me + 1)

    def send(kind, side, source, dest):
        return pltpu.make_async_remote_copy(
            src_ref=source,
            dst_ref=dest,
            send_sem=send_sems.at[kind, side],
            recv_sem=recv_sems.at[kind, side],
            device_id={"lat": target[side]},
            device_id_type=pl.DeviceIdType.MESH,
        )

    def start_both(kind, source, to_high, to_low):
        @pl.when(has[0])
        def _():
            send(kind, 0, source, to_high).start()

        @pl.when(has[1])
        def _():
            send(kind, 1, source, to_low).start()

    def wait_both(kind, source, to_high, to_low):
        @pl.when(has[0])
        def _():
            send(kind, 1, source, to_low).wait_recv()
            send(kind, 0, source, to_high).wait_send()

        @pl.when(has[1])
        def _():
            send(kind, 0, source, to_high).wait_recv()
            send(kind, 1, source, to_low).wait_send()

    loads = (
        pltpu.make_async_copy(qkv_ref, qkv_here, load_sems.at[0]),
        pltpu.make_async_copy(wout_ref, wout_here, load_sems.at[1]),
    )
    for load in loads:
        load.start()
    barrier = pltpu.get_barrier_semaphore()
    for side in range(2):
        @pl.when(has[side])
        def _(side=side):
            pl.semaphore_signal(
                barrier, inc=1, device_id={"lat": target[side]},
                device_id_type=pl.DeviceIdType.MESH,
            )

    @pl.when(jnp.logical_not(has[0]))
    def _():
        surf[0] = jnp.zeros_like(surf[0])
        near[0] = jnp.zeros_like(near[0])
        rows[0] = jnp.zeros_like(rows[0])
        flux_low[...] = jnp.zeros_like(flux_low)

    @pl.when(jnp.logical_not(has[1]))
    def _():
        surf[2] = jnp.zeros_like(surf[2])
        near[2] = jnp.zeros_like(near[2])
        rows[2] = jnp.zeros_like(rows[2])
        flux_high[...] = jnp.zeros_like(flux_high)

    olon = top_ref.shape[1]
    alon = olon // SPAN
    spans = lax.broadcasted_iota(jnp.int32, (olon, alon), 0) // SPAN
    chosen = spans == lax.broadcasted_iota(jnp.int32, (olon, alon), 1)
    mean = jnp.where(chosen, 1.0, 0.0).astype(jnp.bfloat16)
    surf[1] = (
        jnp.dot(top_ref[...], mean, preferred_element_type=jnp.float32) * (1.0 / SPAN)
    ).astype(jnp.bfloat16)
    pl.semaphore_wait(barrier, jnp.where(has[0], 1, 0) + jnp.where(has[1], 1, 0))
    surf_args = (0, surf.at[1], surf.at[2], surf.at[0])
    start_both(*surf_args)
    wait_both(*surf_args)
    band = jnp.zeros((VARS, surf.shape[2]), jnp.float32)
    for part in range(3):
        block = surf[part].astype(jnp.float32)
        for i in range(block.shape[0] // VARS):
            rows_here = block.shape[0] // VARS
            column = (me + part - 1) * rows_here + i
            weight = jnp.float32(0.0)
            for b in range(surf_weight.shape[1]):
                weight = weight + jnp.where(surf_first[0] + b == column, surf_weight[0, b], 0.0)
            weight = jnp.where((column >= 0) & (column < count * rows_here), weight, 0.0)
            band = band + weight * block[i * VARS : (i + 1) * VARS]
    band = jnp.concatenate([band, jnp.zeros_like(band)], axis=0)
    embed = jnp.concatenate([embed_ref[...], jnp.zeros_like(embed_ref[...])], axis=0)
    started = atmos_ref[...].astype(jnp.float32) + lax.dot_general(
        band, embed, (((0,), (0,)), ((), ())), precision=lax.Precision.HIGHEST,
        preferred_element_type=jnp.float32,
    )
    held[...] = started
    near[1] = rms_norm(started, gain_ref[...]).astype(jnp.bfloat16)
    near_args = (1, near.at[1], near.at[2], near.at[0])
    ocean_args = (2, ocean_ref, ocean_high, ocean_low)
    land_args = (5, land_ref, land_high, land_low)
    start_both(*near_args)

    lane = lax.broadcasted_iota(jnp.int32, (1, group), 1) // depth

    def head_scales(raw):
        squares = raw * raw
        factor = jnp.zeros_like(raw)
        for h in range(per_group):
            total = jnp.sum(jnp.where(lane == h, squares, 0.0), axis=1, keepdims=True)
            factor = jnp.where(lane == h, lax.rsqrt(total * (1.0 / depth) + 1e-06), factor)
        return raw * factor

    def project(part, column):
        return jnp.dot(
            near[part], qkv_here[:, pl.ds(pl.multiple_of(column, group), group)],
            preferred_element_type=jnp.float32,
        )

    def head_scores(queries, h, keys):
        query = jnp.where(lane == h, queries, jnp.zeros_like(queries))
        return lax.dot_general(
            query, keys, (((1,), (1,)), ((), ())), preferred_element_type=jnp.float32
        )

    def own(g, carry):
        column = g * group
        query = head_scales(project(1, column))
        scale = jnp.zeros((1, group), jnp.float32)
        for h in range(per_group):
            scale = jnp.where(lane == h, scale_ref[g * per_group + h], scale)
        near_q[g] = (query * (scale * (1.0 / depth**0.5))).astype(jnp.bfloat16)
        near_k[g, 1] = head_scales(project(1, width + column)).astype(jnp.bfloat16)
        near_v[g, 1] = project(1, 2 * width + column).astype(jnp.bfloat16)
        queries = near_q[g]
        mixed = jnp.zeros((token_count, group), jnp.float32)
        for h in range(per_group):
            score = head_scores(queries, h, near_k[g, 1])
            largest = jnp.max(score, axis=1, keepdims=True)
            raised = jnp.exp(score - largest)
            own_largest[g * per_group + h] = largest
            own_total[g * per_group + h] = jnp.sum(raised, axis=1, keepdims=True)
            value = jnp.dot(
                raised.astype(jnp.bfloat16), near_v[g, 1], preferred_element_type=jnp.float32
            )
            mixed = jnp.where(lane == h, value, mixed)
        own_mixed[g] = mixed
        return carry

    loads[0].wait()
    lax.fori_loop(0, groups, own, 0)
    loads[1].wait()
    wait_both(*near_args)
    start_both(*ocean_args)
    start_both(*land_args)

    def attend(g, carry):
        column = g * group
        for part in (0, 2):
            near_k[g, part] = head_scales(project(part, width + column)).astype(jnp.bfloat16)
            near_v[g, part] = project(part, 2 * width + column).astype(jnp.bfloat16)
        queries = near_q[g]
        mixed = jnp.zeros((token_count, group), jnp.float32)
        for h in range(per_group):
            low = jnp.where(has[0], head_scores(queries, h, near_k[g, 0]), -1e30)
            high = jnp.where(has[1], head_scores(queries, h, near_k[g, 2]), -1e30)
            before = own_largest[g * per_group + h]
            largest = jnp.maximum(
                jnp.max(jnp.maximum(low, high), axis=1, keepdims=True), before
            )
            low = jnp.exp(low - largest)
            high = jnp.exp(high - largest)
            fade = jnp.exp(before - largest)
            total = own_total[g * per_group + h] * fade + jnp.sum(low + high, axis=1, keepdims=True)
            value = jnp.dot(
                low.astype(jnp.bfloat16), near_v[g, 0], preferred_element_type=jnp.float32
            ) + jnp.dot(
                high.astype(jnp.bfloat16), near_v[g, 2], preferred_element_type=jnp.float32
            )
            value = (own_mixed[g] * fade + value) * (1.0 / total)
            mixed = jnp.where(lane == h, value, mixed)
        held[...] += jnp.dot(
            mixed.astype(jnp.bfloat16), wout_here[pl.ds(pl.multiple_of(column, group), group), :],
            preferred_element_type=jnp.float32,
        )
        return carry

    lax.fori_loop(0, groups, attend, 0)
    after = held[...]
    after_ref[...] = after.astype(jnp.bfloat16)
    flux_in = rms_norm(after, flux_gain_ref[...]).astype(jnp.bfloat16)
    rows[1] = lax.dot_general(
        wflux_ref[...], flux_in, (((1,), (1,)), ((), ())), preferred_element_type=jnp.float32
    ).astype(jnp.bfloat16)
    rows_args = (3, rows.at[1], rows.at[2], rows.at[0])
    start_both(*rows_args)
    wait_both(*rows_args)
    sources = [rows[part].astype(jnp.float32) for part in range(3)]
    for i in range(flux_mid.shape[0]):
        regridded = jnp.zeros_like(sources[0])
        for part in range(3):
            weight = jnp.float32(0.0)
            for b in range(flux_weight.shape[1]):
                weight = weight + jnp.where(flux_first[i] + b == me + part - 1, flux_weight[i, b], 0.0)
            regridded = regridded + weight * sources[part]
        flux_mid[i] = regridded.astype(jnp.bfloat16)
    flux_args = (4, flux_mid, flux_high, flux_low)
    start_both(*flux_args)
    wait_both(*ocean_args)
    wait_both(*land_args)
    wait_both(*flux_args)


def atmos_block(surf_start, surf_weight, flux_start, flux_weight, head_scale, atmos, top, gain_attn,
                gain_flux, w_qkv, w_out, w_flux, surf_embed, ocean, land_mask):
    token_count, width = atmos.shape
    alon = top.shape[1] // SPAN
    orows = ocean.shape[0]
    nflux = w_flux.shape[1]
    group = 256
    groups = width // group
    vmem = pl.BlockSpec(memory_space=pltpu.VMEM)
    smem = pl.BlockSpec(memory_space=pltpu.SMEM)
    anywhere = pl.BlockSpec(memory_space=pl.ANY)
    flux_shape = jax.ShapeDtypeStruct((orows, nflux, alon), jnp.bfloat16)
    ocean_shape = jax.ShapeDtypeStruct(ocean.shape, ocean.dtype)
    land_shape = jax.ShapeDtypeStruct(land_mask.shape, land_mask.dtype)
    return pl.pallas_call(
        atmos_kernel,
        out_shape=[
            jax.ShapeDtypeStruct((token_count, width), jnp.bfloat16),
            flux_shape, flux_shape, flux_shape, ocean_shape, ocean_shape, land_shape, land_shape,
        ],
        in_specs=[smem] * 5 + [vmem] * 5 + [anywhere] * 2 + [vmem] + [anywhere] * 2,
        out_specs=[vmem] * 4 + [anywhere] * 4,
        scratch_shapes=[
            pltpu.VMEM((3, top.shape[0], alon), jnp.bfloat16),
            pltpu.VMEM((3, token_count, width), jnp.bfloat16),
            pltpu.VMEM((groups, token_count, group), jnp.bfloat16),
            pltpu.VMEM((groups, 3, token_count, group), jnp.bfloat16),
            pltpu.VMEM((groups, 3, token_count, group), jnp.bfloat16),
            pltpu.VMEM((groups, token_count, group), jnp.float32),
            pltpu.VMEM((head_scale.shape[0], token_count, 1), jnp.float32),
            pltpu.VMEM((head_scale.shape[0], token_count, 1), jnp.float32),
            pltpu.VMEM((token_count, width), jnp.float32),
            pltpu.VMEM((3, nflux, alon), jnp.bfloat16),
            pltpu.VMEM(w_qkv.shape, w_qkv.dtype),
            pltpu.VMEM(w_out.shape, w_out.dtype),
            pltpu.SemaphoreType.DMA((2,)),
            pltpu.SemaphoreType.DMA((6, 2)),
            pltpu.SemaphoreType.DMA((6, 2)),
        ],
        compiler_params=pltpu.CompilerParams(
            collective_id=0, has_side_effects=True, vmem_limit_bytes=58 * 1024 * 1024
        ),
        name="atmos_block",
    )(surf_start, surf_weight, flux_start, flux_weight, head_scale, atmos, top, surf_embed,
      gain_attn[None, :], gain_flux[None, :], w_qkv, w_out, w_flux.T, ocean, land_mask)


def ocean_kernel(low_ref, mid_ref, high_ref, land_low, land_mid, land_high,
                 flux_low, flux_mid, flux_high,
                 first_ref, second_ref, out_ref, xs, hs, st, sea):
    och = mid_ref.shape[1]
    olon = mid_ref.shape[2]
    orows = mid_ref.shape[0]
    wide = xs.shape[1]
    nflux = flux_mid.shape[1]
    hid = first_ref.shape[0] // 3
    opad = second_ref.shape[0] // 3
    stride = opad + nflux
    first_row = lax.axis_index("lat") * orows
    total = lax.axis_size("lat") * orows
    alon = flux_mid.shape[2]
    column = lax.broadcasted_iota(jnp.int32, (alon, wide), 1)
    longitude = jnp.where(column < olon, column, jnp.where(column == olon, 0, olon - 1))
    chosen = longitude // SPAN == lax.broadcasted_iota(jnp.int32, (alon, wide), 0)
    repeat = jnp.where(chosen, 1.0, 0.0).astype(jnp.bfloat16)
    tail = wide - 128
    first_pad = olon - tail

    def wrap(head, last):
        lane = lax.broadcasted_iota(jnp.int32, last.shape, 1)
        end = pltpu.roll(last, 128 - first_pad, 1)
        begin = pltpu.roll(head, first_pad, 1)
        return jnp.where(lane == first_pad, begin, jnp.where(lane == 127, end, last))

    def combine(full, size):
        left = pltpu.roll(full[0:size], 1, 1)
        right = pltpu.roll(full[2 * size : 3 * size], wide - 1, 1)
        return left + full[size : 2 * size] + right

    sides = (
        (low_ref, land_low, flux_low), (mid_ref, land_mid, flux_mid), (high_ref, land_high, flux_high)
    )
    for part, (ref, land, flux) in enumerate(sides):
        def fill(i, carry, ref=ref, land=land, flux=flux, part=part):
            row = part * orows + i
            place = first_row + row - orows
            inside = (place >= 0) & (place < total)
            state = jnp.where(inside, ref[i].astype(jnp.float32), 0.0)
            cells = jnp.where(inside, land[pl.ds(i, 1), :].astype(jnp.float32), 0.0)
            sea[row, :, 0:tail] = cells[:, 0:tail]
            sea[row, :, tail:] = jnp.concatenate(
                [cells[:, tail:], jnp.zeros((1, wide - olon), jnp.float32)], axis=1
            )
            state = jnp.concatenate([state, jnp.zeros((opad - och, olon), jnp.float32)], axis=0)
            last = jnp.concatenate(
                [state[:, tail:], jnp.zeros((opad, wide - olon), jnp.float32)], axis=1
            )
            st[row, :, 0:tail] = state[:, 0:tail]
            st[row, :, tail:] = wrap(state[:, 0:128], last)
            base = pl.multiple_of(row * stride, 16)
            xs[pl.ds(base, opad), :] = st[row].astype(jnp.bfloat16)
            spread = jnp.dot(flux[i], repeat, preferred_element_type=jnp.float32)
            base = pl.multiple_of(row * stride + opad, 16)
            xs[pl.ds(base, nflux), :] = spread.astype(jnp.bfloat16)
            return carry
        lax.fori_loop(0, orows, fill, 0)

    for step in range(OSTEPS):
        edge = 1 + 2 * step

        def first(row, carry):
            block = xs[pl.ds(pl.multiple_of((row - 1) * stride, 16), 3 * stride), :]
            full = jnp.dot(first_ref[...], block, preferred_element_type=jnp.float32)
            hidden = jax.nn.gelu(combine(full, hid), approximate=True)
            place = first_row + row - orows
            inside = jnp.where((place >= 0) & (place < total), 1.0, 0.0).astype(jnp.float32)
            hidden = hidden * inside
            base = pl.multiple_of(row * hid, 16)
            hs[pl.ds(base, hid), 0:tail] = hidden[:, 0:tail].astype(jnp.bfloat16)
            hs[pl.ds(base, hid), tail:] = wrap(hidden[:, 0:128], hidden[:, tail:]).astype(jnp.bfloat16)
            return carry
        lax.fori_loop(edge, 3 * orows - edge, first, 0, unroll=2)

        def second(row, carry):
            block = hs[pl.ds(pl.multiple_of((row - 1) * hid, 16), 3 * hid), :]
            full = jnp.dot(second_ref[...], block, preferred_element_type=jnp.float32)
            state = st[row] + sea[row] * combine(full, opad)
            if step == OSTEPS - 1:
                out_ref[row - orows] = state[0:och, 0:olon].astype(jnp.bfloat16)
            else:
                st[row, :, 0:tail] = state[:, 0:tail]
                st[row, :, tail:] = wrap(state[:, 0:128], state[:, tail:])
                base = pl.multiple_of(row * stride, 16)
                xs[pl.ds(base, opad), :] = st[row].astype(jnp.bfloat16)
            return carry
        lax.fori_loop(edge + 1, 3 * orows - edge - 1, second, 0, unroll=4)


def round_up(value, unit):
    return (value + unit - 1) // unit * unit


def ocean_steps(state_parts, land_parts, fluxes, conv_first, conv_second):
    orows, _, olon = state_parts[1].shape
    och = conv_second.shape[1]
    nflux = fluxes[1].shape[1]
    hid = conv_first.shape[1]
    opad = round_up(och, 16)
    wide = round_up(olon + 2, 128)
    first = conv_first.reshape(3, 3, hid, och + nflux)
    first = jnp.concatenate(
        [first[..., :och], jnp.zeros((3, 3, hid, opad - och), first.dtype), first[..., och:]], axis=3
    )
    first = first.transpose(1, 2, 0, 3).reshape(3 * hid, 3 * (opad + nflux))
    second = jnp.pad(conv_second.reshape(3, 3, och, hid), ((0, 0), (0, 0), (0, opad - och), (0, 0)))
    second = second.transpose(1, 2, 0, 3).reshape(3 * opad, 3 * hid)
    vmem = pl.BlockSpec(memory_space=pltpu.VMEM)
    return pl.pallas_call(
        ocean_kernel,
        out_shape=jax.ShapeDtypeStruct((orows, och, olon), jnp.bfloat16),
        in_specs=[vmem] * 11,
        out_specs=vmem,
        scratch_shapes=[
            pltpu.VMEM((3 * orows * (opad + nflux), wide), jnp.bfloat16),
            pltpu.VMEM((3 * orows * hid, wide), jnp.bfloat16),
            pltpu.VMEM((3 * orows, opad, wide), jnp.float32),
            pltpu.VMEM((3 * orows, 1, wide), jnp.float32),
        ],
        compiler_params=pltpu.CompilerParams(vmem_limit_bytes=60 * 1024 * 1024),
        name="ocean_steps",
    )(*state_parts, *land_parts, *fluxes, first, second)


def local(
    atmos,
    ocean_state,
    land_mask,
    w_qkv,
    w_out,
    head_scale,
    gain_attn,
    gain_flux,
    w_flux,
    surf_embed,
    flux_start,
    flux_weight,
    surf_start,
    surf_weight,
    conv_first,
    conv_second,
):
    orows = ocean_state.shape[1]
    ocean = ocean_state.transpose(1, 0, 2)
    top = ocean_state[::LEVELS].transpose(1, 0, 2).reshape(orows * VARS, -1)
    outs = atmos_block(
        surf_start, surf_weight, flux_start, flux_weight, head_scale, atmos, top, gain_attn,
        gain_flux, w_qkv, w_out, w_flux, surf_embed, ocean, land_mask,
    )
    atmos_next, flux_mid, flux_low, flux_high, ocean_low, ocean_high, land_low, land_high = outs
    ocean_next = ocean_steps(
        [ocean_low, ocean, ocean_high], [land_low, land_mask, land_high],
        [flux_low, flux_mid, flux_high], conv_first, conv_second,
    )
    return (atmos_next, ocean_next.transpose(1, 0, 2))


def solution(mesh):
    in_specs = (
        P(("ens", "lat"), None),
        P(None, ("ens", "lat"), None),
        P("lat", None),
        P(),
        P(),
        P(),
        P(),
        P(),
        P(),
        P(),
        P("lat"),
        P("lat", None),
        P("lat"),
        P("lat", None),
        P(),
        P(),
    )
    out_specs = (P(("ens", "lat"), None), P(None, ("ens", "lat"), None))
    return jax.shard_map(local, mesh=mesh, in_specs=in_specs, out_specs=out_specs, check_vma=False)
```
